256 devices in a mesh: rows: 64 (over z, y, core), cols: 4 (over x).
Axes of the slice: x: 4, y: 4, z: 8, core: 2. Of those that a mesh axis runs over, the one named last changes fastest.
Arguments:
- features: bfloat16 [65536, 256], P(('rows', 'cols')), may hold values from -6 to 6
- weight: bfloat16 [256, 256], replicated, may hold values from -0.375 to 0.375
- bias: float32 [256], replicated, may hold values from -3 to 3
- tile_values: bfloat16 [64, 4, 64, 3, 128, 128], P('rows', 'cols'), may hold values from -0.078125 to 0.078125
- tile_source: int32 [64, 4, 64, 3], P('rows', 'cols'), may hold values from 0 to 7
- tile_dest: int32 [64, 4, 64, 3], P('rows', 'cols'), may hold values from 0 to 1
- send_counts: int32 [64, 4, 64], P('rows', 'cols'), may hold values from 0 to 3, as said below
- cotangent: bfloat16 [65536, 256], P(('rows', 'cols')), may hold values from -6 to 6
Outputs:
- output: bfloat16 [65536, 256], P(('rows', 'cols'))
- input_grad: bfloat16 [65536, 256], P(('rows', 'cols'))
- weight_grad: float32 [256, 256], replicated
- bias_grad: float32 [256], replicated
The draws below stay inside these ranges and needn't reach their ends.
Inputs may be any that keep to these rules, and one draw needn't show every extreme that they name: `send_counts`: in each column group one owner, drawn from the seed, receives 3 live slots from every sender.
All inputs are finite; a program needn't handle non-finite values.
Results may differ from the reference program's by a relative error of at most 0.014.
Values may be sent and summed in bfloat16 or wider, within the bound.
A program may use at most 128 MiB of HBM per device.

```python
import jax
import jax.numpy as jnp
from jax import lax

F = 256
TILE = 128
TD = 2
CAP = 3
NODES = 65536
N_ROWS = 64
N_COLS = 4


def draw_send_counts(key, part):
    key_base, key_full = jax.random.split(jax.random.fold_in(key, 17))
    base_counts = jax.random.randint(key_base, (N_ROWS, N_COLS, N_ROWS), 0, CAP + 1)
    full_owner = jax.random.randint(key_full, (N_COLS,), 0, N_ROWS)
    owner_hit = full_owner[None, :, None] == jnp.arange(N_ROWS)[None, None, :]
    return jnp.where(owner_hit, CAP, base_counts).astype(jnp.int32)


def plant(drawn, own_key, smallest, largest):
    shape = drawn.shape
    index_at = [jax.random.randint(jax.random.fold_in(own_key, axis), (), 0, shape[axis]) for axis in range(len(shape))]
    drawn = drawn.at[tuple(index_at)].set(smallest)
    longest = shape.index(max(shape))
    index_at[longest] = (index_at[longest] + 1) % shape[longest]
    return drawn.at[tuple(index_at)].set(largest)


def steps_of(rng, dims, cuts, smallest, top_value):
    gain, own = 1.0, jax.random.fold_in(rng, 6)
    for position, parts in cuts:
        steps = jnp.exp(jax.random.uniform(jax.random.fold_in(own, position), (parts,), jnp.float32, smallest / len(cuts), top_value / len(cuts)))
        gain = gain * jnp.repeat(steps, dims[position] // parts).reshape([-1 if axis == position else 1 for axis in range(len(dims))])
    return gain


def scatter_about(own_key, dims, scale, limit, shards=(), kind=jnp.bfloat16):
    values = scale * jax.random.normal(own_key, dims, jnp.float32)
    if shards:
        values = values * steps_of(own_key, dims, shards, -0.22, 0.18)
    return jnp.clip(values, -limit, limit).astype(kind)


def setup_inputs(seed: int = 0) -> dict:
    splits = jax.random.split(jax.random.key(seed), 9)
    features = scatter_about(splits[0], (NODES, F), 1.0, 6.0, ((0, 256),))
    weight = scatter_about(splits[1], (F, F), F ** -0.5, 0.375)
    bias = scatter_about(splits[2], (F,), 0.5, 3.0, (), jnp.float32)
    tile_values = scatter_about(splits[3], (N_ROWS, N_COLS, N_ROWS, CAP, TILE, TILE), (TILE * N_ROWS * CAP // (2 * TD)) ** -0.5, 0.078125, ((0, 64), (1, 4)))
    tile_source = plant(jax.random.randint(splits[4], (N_ROWS, N_COLS, N_ROWS, CAP), 0, N_COLS * TD), jax.random.fold_in(splits[4], 1), 0, (N_COLS * TD) - 1).astype(jnp.int32)
    tile_dest = plant(jax.random.randint(splits[5], (N_ROWS, N_COLS, N_ROWS, CAP), 0, TD), jax.random.fold_in(splits[5], 1), 0, TD - 1).astype(jnp.int32)
    send_counts = draw_send_counts(jax.random.fold_in(splits[8], 71), 0)
    cotangent = scatter_about(splits[7], (NODES, F), 1.0, 6.0, ((0, 256),))
    return dict(features=features, weight=weight, bias=bias, tile_values=tile_values, tile_source=tile_source, tile_dest=tile_dest, send_counts=send_counts, cotangent=cotangent)


def reference(features, weight, bias, tile_values, tile_source, tile_dest, send_counts, cotangent):
    width = weight.shape[1]
    hidden = jnp.dot(features, weight, preferred_element_type=jnp.float32).astype(jnp.bfloat16)
    block_tiles = hidden.reshape(N_ROWS, N_COLS * TD, TILE, width)
    slot_ids = jnp.arange(CAP, dtype=jnp.int32)
    dest_ids = jnp.arange(TD, dtype=jnp.int32)
    span_ids = jnp.arange(N_COLS * TD, dtype=jnp.int32)
    owner_ids = jnp.arange(N_ROWS, dtype=jnp.int32)

    def device_data(device_step):
        row_index = device_step // N_COLS
        col_index = device_step % N_COLS
        live_slots = (slot_ids[None, :] < send_counts[row_index, col_index][:, None]).astype(jnp.float32)
        tile_vals = tile_values[row_index, col_index].astype(jnp.float32)
        return (row_index, col_index, tile_vals, tile_source[row_index, col_index], tile_dest[row_index, col_index], live_slots)

    def push_step(running, device_step):
        row_index, col_index, tile_vals, source_ids, target_ids, live_slots = device_data(device_step)
        chosen = block_tiles[row_index][source_ids].astype(jnp.float32)
        partial_tiles = jnp.einsum('osab,osaf->osbf', tile_vals, chosen)
        routing = (target_ids[:, :, None] == dest_ids[None, None, :]).astype(jnp.float32) * live_slots[:, :, None]
        contrib = jnp.einsum('ost,osbf->otbf', routing, partial_tiles).astype(jnp.bfloat16)
        return (running.at[:, col_index].add(contrib.astype(jnp.float32)), None)
    steps_all = jnp.arange(N_ROWS * N_COLS, dtype=jnp.int32)
    start_sum = jnp.zeros((N_ROWS, N_COLS, TD, TILE, width), jnp.float32)
    summed, _ = lax.scan(push_step, start_sum, steps_all)
    pre = summed.reshape(-1, width) + bias.astype(jnp.float32)[None, :]
    output = jax.nn.gelu(pre).astype(jnp.bfloat16)
    _, backward_fn = jax.vjp(jax.nn.gelu, pre)
    grad_pre = backward_fn(cotangent.astype(jnp.float32))[0].astype(jnp.bfloat16)
    grad_tiles = grad_pre.reshape(N_ROWS, N_COLS, TD, TILE, width)

    def pull_step(running, device_step):
        row_index, col_index, tile_vals, source_ids, target_ids, live_slots = device_data(device_step)
        column_grads = grad_tiles[:, col_index]
        chosen = column_grads[owner_ids[:, None], target_ids].astype(jnp.float32)
        term = jnp.einsum('osab,osbf->osaf', tile_vals, chosen) * live_slots[:, :, None, None]
        spread = (source_ids[:, :, None] == span_ids[None, None, :]).astype(jnp.float32)
        piece_sum = jnp.einsum('osj,osaf->jaf', spread, term)
        return (running.at[row_index].add(piece_sum), None)
    start_grad = jnp.zeros((N_ROWS, N_COLS * TD, TILE, width), jnp.float32)
    grad_sum, _ = lax.scan(pull_step, start_grad, steps_all)
    grad_rounded = grad_sum.reshape(-1, width).astype(jnp.bfloat16)
    input_grad = jnp.dot(grad_rounded, weight.T, preferred_element_type=jnp.float32).astype(jnp.bfloat16)
    scale_factor = 1.0 / jnp.sqrt(jnp.float32(NODES))
    weight_grad = jnp.dot(features.T, grad_rounded, preferred_element_type=jnp.float32) * scale_factor
    bias_grad = lax.optimization_barrier(jnp.sum(grad_pre.astype(jnp.float32), axis=0)) * scale_factor
    return (output, input_grad, weight_grad, bias_grad)
```

```python
import math

import jax
import jax.numpy as jnp
from jax import lax
from jax.experimental import pallas as pl
from jax.experimental.pallas import tpu as pltpu
from jax.sharding import PartitionSpec as P

MESH = pl.DeviceIdType.MESH
BF = jnp.bfloat16
F32 = jnp.float32
NK = 2
NY = 4
VMEM_LIMIT = 62 * 1024 * 1024

RATE = {"x": 46e3, "y": 46e3, "z": 46e3, "k": 300e3}
DELAY = {"x": 2.4, "y": 1.7, "z": 1.7, "k": 1.0}


class Flow:
    def __init__(self):
        self.events = []
        self.msgs = {}

    def msg(self, name, link, nbytes, src, dst, view, peer):
        self.msgs[name] = dict(idx=len(self.msgs), link=link, nbytes=nbytes, src=src, dst=dst, view=view, peer=peer)

    def event(self, name, needs, fn=None, sends=(), cost=0.15):
        self.events.append((name, tuple(needs), fn, tuple(sends), cost))

    def order(self):
        done, free, now, out = {}, {}, 0.0, []
        pending = list(self.events)
        while pending:
            best = None
            for pos, ev in enumerate(pending):
                if all(n in done for n in ev[1]):
                    ready = max([now] + [done[n] for n in ev[1]])
                    if best is None or ready < best[0] - 1e-9:
                        best = (ready, pos)
            ready, pos = best
            ev = pending.pop(pos)
            now = ready + ev[4]
            done[ev[0]] = now
            for s in ev[3]:
                m = self.msgs[s]
                end = max(now, free.get(m["link"], 0.0)) + m["nbytes"] / RATE[m["link"][0]]
                free[m["link"]] = end
                done[s] = end + DELAY[m["link"][0]]
            out.append(ev)
        self.total = now
        return out

    def emit(self, send_sem, recv_sem):
        waited = set()

        def copy(m):
            return pltpu.make_async_remote_copy(
                src_ref=m["src"](), dst_ref=m["dst"](), send_sem=send_sem.at[m["idx"]],
                recv_sem=recv_sem.at[m["idx"]], device_id=m["peer"], device_id_type=MESH)

        for name, needs, fn, sends, _ in self.order():
            for n in needs:
                if n in self.msgs and n not in waited:
                    waited.add(n)
                    m = self.msgs[n]
                    v = m["view"]()
                    pltpu.make_async_remote_copy(
                        src_ref=v, dst_ref=v, send_sem=send_sem.at[m["idx"]],
                        recv_sem=recv_sem.at[m["idx"]], device_id=m["peer"], device_id_type=MESH).wait_recv()
            if fn is not None:
                fn()
            for s in sends:
                copy(self.msgs[s]).start()
        for n, m in self.msgs.items():
            copy(m).wait_send()


def greet(peers):
    barrier = pltpu.get_barrier_semaphore()
    for peer in peers:
        pl.semaphore_signal(barrier, inc=1, device_id=peer, device_id_type=MESH)
    pl.semaphore_wait(barrier, len(peers))


def mod(v, n):
    return lax.rem(v + 2 * n, n)


def main_kernel(dims, feat, weight, bias, tiles, src_ids, dst_ids, counts, cot,
                out, ga, wg, bg,
                av, xf, xt, psend, precv, own0, own1, r0, r1, s0, s1, qt,
                w1, w1r, w2, w2r, w3, w3r, w4r, wtot, send_sem, recv_sem, load_sem):
    nz, ncols, tile, width, scale = dims
    cap = av.shape[1]
    r = lax.axis_index("rows")
    c = lax.axis_index("cols")
    k = lax.rem(r, NK)
    y = lax.rem(lax.div(r, NK), NY)
    z = lax.div(r, NK * NY)
    hz, hy = nz // 2, NY // 2
    per_core = nz * NY

    def rid(zz, yy, kk):
        return (zz * NY + yy) * NK + kk

    def zdev(o):
        return (rid(mod(z + o, nz), y, k), c)

    def ydev(o):
        return (rid(z, mod(y + o, NY), k), c)

    def xdev(o):
        return (r, mod(c + o, ncols))

    partner = (rid(z, y, 1 - k), c)

    zord = [hz] + [s * d for d in range(hz - 1, 0, -1) for s in (1, -1)] + [0]
    yord = [hy] + [s * d for d in range(hy - 1, 0, -1) for s in (1, -1)] + [0]

    def load(i):
        zz = mod(z + zord[i], nz)
        blk = pl.ds(zz * NY * NK, NY * NK)
        return pltpu.make_async_copy(tiles.at[blk], av.at[blk], load_sem.at[i])

    for i in range(nz):
        load(i).start()

    greet([zdev(o) for o in range(1, nz)] + [ydev(o) for o in range(1, NY)]
          + [xdev(o) for o in range(1, ncols)] + [partner])

    flow = Flow()

    for o in range(1, ncols):
        flow.msg(f"ax{o}", "x", tile * 2 * width * 2 * 1.33,
                 lambda: feat, lambda: xf.at[c], lambda o=o: xf.at[mod(c - o, ncols)], xdev(o))

    def keep_own():
        xf[c] = feat[...]

    flow.event("ax", (), keep_own, [f"ax{o}" for o in range(1, ncols)])

    def turn():
        for j in range(ncols):
            for h in range(2):
                xt[2 * j + h] = xf[j, h * tile:(h + 1) * tile, :].T

    flow.event("xt", ["ax"] + [f"ax{o}" for o in range(1, ncols)], turn, cost=1.0)

    def partial_tile(o):
        lhs, rhs = [], []
        cnt = counts[o]
        for s in range(cap):
            t = dst_ids[o, s]
            live = jnp.where(s < cnt, 1, 0)
            m1 = (live * t).astype(F32)
            m0 = (live * (1 - t)).astype(F32)
            a = av[o, s]
            lhs.append(xt[src_ids[o, s]])
            rhs.append(jnp.concatenate(
                [a * jnp.full((tile, tile), m0, F32).astype(BF),
                 a * jnp.full((tile, tile), m1, F32).astype(BF)], axis=1))
        return jnp.dot(jnp.concatenate(lhs, axis=1), jnp.concatenate(rhs, axis=0),
                       preferred_element_type=F32).astype(BF)

    def forward(i):
        zz = mod(z + zord[i], nz)
        load(i).wait()

        def body(j, carry):
            theirs = partial_tile(rid(zz, j, 1 - k))
            psend[zz, j, 0] = theirs[:, :tile]
            psend[zz, j, 1] = theirs[:, tile:]
            mine = partial_tile(rid(zz, j, k))
            own0[zz, j] = mine[:, :tile]
            own1[j, zz] = mine[:, tile:]
            return carry

        lax.fori_loop(0, NY, body, 0)

    for i in range(nz):
        zat = lambda i=i: mod(z + zord[i], nz)
        flow.msg(f"pe{i}", "k", NY * 2 * width * tile * 2,
                 lambda f=zat: psend.at[f()], lambda f=zat: precv.at[f()], lambda f=zat: precv.at[f()], partner)
        flow.event(f"fw{i}", ["xt"] + ([f"fw{i - 1}"] if i else []), lambda i=i: forward(i), [f"pe{i}"], cost=1.0)

    halves = {1: pl.ds(0, width // 2), -1: pl.ds(width // 2, width // 2)}

    def chain(tag, n, link, dev, items, buf, extra, rbuf, ready, final):
        h = n // 2
        piece = width * tile * 2

        def rview(i, d, q, rows=None):
            v = rbuf.at[0 if d > 0 else 1, i, q]
            return v if rows is None else v.at[rows]

        def combine(off, it, recvs):
            for d in (1, -1):
                rows = halves[d]
                v = buf(off, it)[rows, :].astype(F32)
                e = extra(off, it) if extra is not None else None
                if e is not None:
                    v = v + e[rows, :].astype(F32)
                for (i, rd, q) in recvs:
                    if i > 0 or rd == d:
                        v = v + rview(i, rd, q)[rows, :].astype(F32)
                yield rows, v

        def store(off, it, recvs):
            dst = buf(off, it)
            for rows, v in combine(off, it, recvs):
                dst[rows, :] = v.astype(BF)

        for q, it in enumerate(items):
            for i in range(h):
                for d in (1, -1):
                    off = d * (h - i)
                    rows = halves[d] if i == 0 else None

                    def src(off=off, it=it, rows=rows):
                        v = buf(off, it)
                        return v if rows is None else v.at[rows]

                    def dst(i=i, d=d, q=q, rows=rows):
                        return rview(i, d, q, rows)

                    flow.msg(f"{tag}.{i}.{d}.{q}", link + ("+" if d > 0 else "-"),
                             piece // 2 if i == 0 else piece, src, dst, dst, dev(d))
            if extra is not None:
                flow.event(f"{tag}.s0.{q}", ready(h, it), lambda it=it: store(h, it, ()),
                           [f"{tag}.0.1.{q}", f"{tag}.0.-1.{q}"])
            else:
                flow.event(f"{tag}.s0.{q}", ready(h, it), None, [f"{tag}.0.1.{q}", f"{tag}.0.-1.{q}"], cost=0.02)
            for i in range(1, h):
                for d in (1, -1):
                    off = d * (h - i)
                    flow.event(f"{tag}.s{i}.{d}.{q}", list(ready(off, it)) + [f"{tag}.{i - 1}.{d}.{q}"],
                               lambda off=off, it=it, i=i, d=d, q=q: store(off, it, [(i - 1, d, q)]),
                               [f"{tag}.{i}.{d}.{q}"])

            def finish(it=it, q=q):
                recvs = [(h - 1, 1, q), (h - 1, -1, q)]
                if final is None:
                    store(0, it, recvs)
                else:
                    for rows, v in combine(0, it, recvs):
                        final[rows, :] = v

            flow.event(f"{tag}.fin.{q}", list(ready(0, it)) + [f"{tag}.{h - 1}.1.{q}", f"{tag}.{h - 1}.-1.{q}"], finish)

    def zpos(off):
        return [i for i, v in enumerate(zord) if (v - off) % nz == 0][0]

    def ypos(off):
        return [i for i, v in enumerate(yord) if (v - off) % NY == 0][0]

    chain("a1", nz, "z", zdev, yord,
          lambda off, dy: own0.at[mod(z + off, nz), mod(y + dy, NY)],
          lambda off, dy: precv.at[mod(z + off, nz), mod(y + dy, NY), 0],
          r0, lambda off, dy: [f"fw{zpos(off)}", f"pe{zpos(off)}"], None)
    chain("b1", NY, "y", ydev, zord,
          lambda off, dz: own1.at[mod(y + off, NY), mod(z + dz, nz)],
          lambda off, dz: precv.at[mod(z + dz, nz), mod(y + off, NY), 1],
          r1, lambda off, dz: [f"fw{zpos(dz)}", f"pe{zpos(dz)}"], None)
    chain("b2", nz, "z", zdev, [0],
          lambda off, it: own1.at[y, mod(z + off, nz)],
          None, s1, lambda off, it: [f"b1.fin.{zpos(off)}"], qt.at[1])
    chain("a2", NY, "y", ydev, [0],
          lambda off, it: own0.at[z, mod(y + off, NY)],
          None, s0, lambda off, it: [f"a1.fin.{ypos(off)}"], qt.at[0])

    slot0 = lambda kk, zz, yy: kk * per_core + zz * NY + yy
    slot1 = lambda kk, zz, yy: (NK + kk) * per_core + yy * nz + zz

    def activate():
        wb = weight[...]
        q = jnp.concatenate([qt[0], qt[1]], axis=1)
        qh = q.astype(BF)
        ql = (q - qh.astype(F32)).astype(BF)
        dn = (((0,), (0,)), ((), ()))
        pre = (lax.dot_general(qh, wb, dn, preferred_element_type=F32)
               + lax.dot_general(ql, wb, dn, preferred_element_type=F32) + bias[...])
        ks = math.sqrt(2.0 / math.pi)
        sq = pre * pre
        th = jnp.tanh(ks * pre * (1.0 + 0.044715 * sq))
        out[...] = (0.5 * pre * (1.0 + th)).astype(BF)
        slope = 0.5 * (1.0 + th) + 0.5 * pre * (1.0 - th * th) * (ks * (1.0 + 3 * 0.044715 * sq))
        g = (cot[...].astype(F32) * slope).astype(BF)
        ga[slot0(k, z, y)] = g[:tile]
        ga[slot1(k, z, y)] = g[tile:]

    flow.event("act", ["a2.fin.0", "b2.fin.0"], activate, cost=1.5)

    ghalf = {1: pl.ds(0, tile // 2), -1: pl.ds(tile // 2, tile // 2)}

    def gather(tag, n, link, dev, items, slot, ready):
        h = n // 2
        piece = tile * width * 2

        def view(off, it, rows):
            v = ga.at[slot(off, it)]
            return v if rows is None else v.at[rows]

        for q, it in enumerate(items):
            for i in range(h):
                for d in (1, -1):
                    rows = ghalf[d] if i == h - 1 else None
                    flow.msg(f"{tag}.{i}.{d}.{q}", link + ("+" if d > 0 else "-"),
                             piece // 2 if i == h - 1 else piece,
                             lambda i=i, d=d, it=it, rows=rows: view(-i * d, it, rows),
                             lambda i=i, d=d, it=it, rows=rows: view(-i * d, it, rows),
                             lambda i=i, d=d, it=it, rows=rows: view(-(i + 1) * d, it, rows), dev(d))
            flow.event(f"{tag}.s.{q}", ready(it), None, [f"{tag}.0.1.{q}", f"{tag}.0.-1.{q}"], cost=0.02)
            for i in range(h - 1):
                for d in (1, -1):
                    flow.event(f"{tag}.f{i}.{d}.{q}", [f"{tag}.{i}.{d}.{q}"], None, [f"{tag}.{i + 1}.{d}.{q}"], cost=0.02)
            flow.event(f"{tag}.last.{q}", [f"{tag}.{h - 1}.1.{q}", f"{tag}.{h - 1}.-1.{q}"], None, cost=0.02)

        def have(off, q, own):
            off = off % n
            if off == 0:
                return own
            if off == h:
                return f"{tag}.last.{q}"
            return f"{tag}.f{off - 1}.-1.{q}" if off < h else f"{tag}.f{n - off - 1}.1.{q}"

        return have

    have_a1 = gather("ga1", NY, "y", ydev, [0],
                     lambda off, it: slot0(k, z, mod(y + off, NY)), lambda it: ["act"])
    have_b1 = gather("gb1", nz, "z", zdev, [0],
                     lambda off, it: slot1(k, mod(z + off, nz), y), lambda it: ["act"])
    near_y, near_z = yord[::-1], zord[::-1]
    have_a2 = gather("ga2", nz, "z", zdev, near_y,
                     lambda off, dy: slot0(k, mod(z + off, nz), mod(y + dy, NY)),
                     lambda dy: [have_a1(dy, 0, "act")])
    have_b2 = gather("gb2", NY, "y", ydev, near_z,
                     lambda off, dz: slot1(k, mod(z + dz, nz), mod(y + off, NY)),
                     lambda dz: [have_b1(dz, 0, "act")])
    ends = []
    for off in near_z:
        needs = [have_a2(off, q, have_a1(dy, 0, "act")) for q, dy in enumerate(near_y)]
        mine = lambda off=off: ga.at[pl.ds(slot0(k, mod(z + off, nz), 0), NY)]
        other = lambda off=off: ga.at[pl.ds(slot0(1 - k, mod(z + off, nz), 0), NY)]
        flow.msg(f"ka{off}", "k", NY * tile * width * 2, mine, mine, other, partner)
        flow.event(f"kas{off}", needs, None, [f"ka{off}"], cost=0.02)
        ends.append(f"ka{off}")
    for off in near_y:
        needs = [have_b2(off, q, have_b1(dz, 0, "act")) for q, dz in enumerate(near_z)]
        mine = lambda off=off: ga.at[pl.ds(slot1(k, 0, mod(y + off, NY)), nz)]
        other = lambda off=off: ga.at[pl.ds(slot1(1 - k, 0, mod(y + off, NY)), nz)]
        flow.msg(f"kb{off}", "k", nz * tile * width * 2, mine, mine, other, partner)
        flow.event(f"kbs{off}", needs, None, [f"kb{off}"], cost=0.02)
        ends.append(f"kb{off}")

    rx, ry, rk = width // ncols, width // ncols // NY, width // ncols // NY // NK

    def wpart():
        q = jnp.concatenate([qt[0], qt[1]], axis=1).astype(BF)
        g = jnp.concatenate([ga[slot0(k, z, y)], ga[slot1(k, z, y)]], axis=0)
        w = jnp.dot(q, g, preferred_element_type=F32)
        b = jnp.broadcast_to(jnp.sum(g.astype(F32), axis=0, keepdims=True), (8, width))
        for j in range(ncols):
            w1[j, :rx] = w[j * rx:(j + 1) * rx]
            w1[j, rx:] = b
        w1r[c] = w1[c]

    for o in range(1, ncols):
        flow.msg(f"w1.{o}", "x", (rx + 8) * width * 4,
                 lambda o=o: w1.at[mod(c + o, ncols)], lambda: w1r.at[c], lambda o=o: w1r.at[mod(c - o, ncols)], xdev(o))
    flow.event("w1", ["act", "ga1.s.0", "gb1.s.0"], wpart, [f"w1.{o}" for o in range(1, ncols)], cost=0.8)

    def wsum2():
        t = w1r[0]
        for j in range(1, ncols):
            t = t + w1r[j]
        for j in range(NY):
            w2[j, :ry] = t[j * ry:(j + 1) * ry]
            w2[j, ry:] = t[rx:]
        w2r[y] = w2[y]

    for o in range(1, NY):
        flow.msg(f"w2.{o}", "y+", (ry + 8) * width * 4,
                 lambda o=o: w2.at[mod(y + o, NY)], lambda: w2r.at[y], lambda o=o: w2r.at[mod(y - o, NY)], ydev(o))
    flow.event("w2", ["w1"] + [f"w1.{o}" for o in range(1, ncols)], wsum2, [f"w2.{o}" for o in range(1, NY)])

    def wsum3():
        t = w2r[0]
        for j in range(1, NY):
            t = t + w2r[j]
        for j in range(NK):
            w3[j, :rk] = t[j * rk:(j + 1) * rk]
            w3[j, rk:] = t[ry:]
        w3r[k] = w3[k]

    flow.msg("w3", "k", (rk + 8) * width * 4, lambda: w3.at[1 - k], lambda: w3r.at[k], lambda: w3r.at[1 - k], partner)
    flow.event("w3s", ["w2"] + [f"w2.{o}" for o in range(1, NY)], wsum3, ["w3"])

    def wsum4():
        w4r[z] = w3r[0] + w3r[1]

    for o in range(1, nz):
        flow.msg(f"w4.{o}", "z+", (rk + 8) * width * 4,
                 lambda: w4r.at[z], lambda: w4r.at[z], lambda o=o: w4r.at[mod(z - o, nz)], zdev(o))
    flow.event("w4s", ["w3s", "w3"], wsum4, [f"w4.{o}" for o in range(1, nz)])

    def wsum5():
        t = w4r[0]
        for j in range(1, nz):
            t = t + w4r[j]
        t = t * scale
        wtot[c, y, k] = t[:rk]
        bg[...] = t[rk:rk + 1]

    flow.msg("w5", "k", rk * width * 4, lambda: wtot.at[c, y, k], lambda: wtot.at[c, y, k],
             lambda: wtot.at[c, y, 1 - k], partner)
    flow.event("w5s", ["w4s"] + [f"w4.{o}" for o in range(1, nz)], wsum5, ["w5"])
    for o in range(1, NY):
        flow.msg(f"w6.{o}", "y+", ry * width * 4, lambda: wtot.at[c, y], lambda: wtot.at[c, y],
                 lambda o=o: wtot.at[c, mod(y - o, NY)], ydev(o))
    flow.event("w6s", ["w5s", "w5"], None, [f"w6.{o}" for o in range(1, NY)])
    for o in range(1, ncols):
        flow.msg(f"w7.{o}", "x", rx * width * 4, lambda: wtot.at[c], lambda: wtot.at[c],
                 lambda o=o: wtot.at[mod(c - o, ncols)], xdev(o))
    flow.event("w7s", ["w6s"] + [f"w6.{o}" for o in range(1, NY)], None, [f"w7.{o}" for o in range(1, ncols)])

    def wend():
        for a in range(ncols):
            for b in range(NY):
                for e in range(NK):
                    base = a * rx + b * ry + e * rk
                    wg[base:base + rk] = wtot[a, b, e]

    flow.event("wend", ["w7s"] + [f"w7.{o}" for o in range(1, ncols)], wend)
    flow.event("end", ends + ["wend"])
    flow.emit(send_sem, recv_sem)


N_MSGS = 400


def backward_kernel(dims, per_step, src_ids, dst_ids, counts, tiles, ga, out, acc):
    nz = dims[0]
    step = pl.program_id(0)
    cap = tiles.shape[1]
    per_core = nz * NY

    @pl.when(step == 0)
    def _():
        acc[...] = jnp.zeros_like(acc)

    terms = []
    for j in range(per_step):
        o = step * per_step + j
        kk = lax.rem(o, NK)
        yy = lax.rem(lax.div(o, NK), NY)
        zz = lax.div(o, NK * NY)
        i0 = kk * per_core + zz * NY + yy
        i1 = (NK + kk) * per_core + yy * nz + zz
        cnt = counts[o]
        for s in range(cap):
            idx = jnp.where(dst_ids[o, s] == 0, i0, i1)
            live = jnp.where(s < cnt, 1, 0).astype(F32)
            a = tiles[j, s] * jnp.full(tiles.shape[2:], live, F32).astype(BF)
            terms.append((src_ids[o, s], jnp.dot(a, ga[idx], preferred_element_type=F32)))
    for j, t in terms:
        acc[j] += t

    @pl.when(step == pl.num_programs(0) - 1)
    def _():
        out[...] = acc[...].astype(BF)


def spread_kernel(ncols, part, weight, out, recv, send_sem, recv_sem):
    r = lax.axis_index("rows")
    c = lax.axis_index("cols")
    peers = [(r, mod(c + o, ncols)) for o in range(1, ncols)]
    greet(peers)
    copies = []
    for o in range(1, ncols):
        cp = pltpu.make_async_remote_copy(
            src_ref=part.at[mod(c + o, ncols)], dst_ref=recv.at[o - 1], send_sem=send_sem.at[o - 1],
            recv_sem=recv_sem.at[o - 1], device_id=peers[o - 1], device_id_type=MESH)
        cp.start()
        copies.append(cp)
    total = part[c].astype(F32)
    for o in range(1, ncols):
        copies[o - 1].wait_recv()
        total = total + recv[o - 1].astype(F32)
    grad = total.astype(BF)
    out[...] = lax.dot_general(grad, weight[...], (((1,), (1,)), ((), ())), preferred_element_type=F32).astype(BF)
    for cp in copies:
        cp.wait_send()


def solution(mesh):
    nrows, ncols = mesh.shape["rows"], mesh.shape["cols"]
    nz = nrows // (NK * NY)
    vmem = pl.BlockSpec(memory_space=pltpu.VMEM)
    smem = pl.BlockSpec(memory_space=pltpu.SMEM)
    anym = pl.BlockSpec(memory_space=pl.ANY)

    def local(features, weight, bias, tile_values, tile_source, tile_dest, send_counts, cotangent):
        owners, cap, tile = tile_values.shape[2:5]
        nodes, width = features.shape
        scale = 1.0 / math.sqrt(nodes * nrows * ncols)
        dims = (nz, ncols, tile, width, scale)
        tiles = tile_values.reshape(owners, cap, tile, tile)
        src_ids = tile_source.reshape(owners, cap)
        dst_ids = tile_dest.reshape(owners, cap)
        counts = send_counts.reshape(owners)
        rx = width // ncols
        ry, rk = rx // NY, rx // NY // NK
        hz, hy = nz // 2, NY // 2

        def body(*refs):
            main_kernel(dims, *refs)

        out, ga, wg, bg = pl.pallas_call(
            body,
            name="graph_main",
            out_shape=(
                jax.ShapeDtypeStruct((nodes, width), BF),
                jax.ShapeDtypeStruct((2 * nrows, tile, width), BF),
                jax.ShapeDtypeStruct((width, width), F32),
                jax.ShapeDtypeStruct((1, width), F32),
            ),
            in_specs=[vmem, vmem, vmem, anym, smem, smem, smem, vmem],
            out_specs=(vmem, vmem, vmem, vmem),
            scratch_shapes=[
                pltpu.VMEM((owners, cap, tile, tile), BF),
                pltpu.VMEM((ncols, nodes, width), BF),
                pltpu.VMEM((2 * ncols, width, tile), BF),
                pltpu.VMEM((nz, NY, 2, width, tile), BF),
                pltpu.VMEM((nz, NY, 2, width, tile), BF),
                pltpu.VMEM((nz, NY, width, tile), BF),
                pltpu.VMEM((NY, nz, width, tile), BF),
                pltpu.VMEM((2, hz, NY, width, tile), BF),
                pltpu.VMEM((2, hy, nz, width, tile), BF),
                pltpu.VMEM((2, hy, 1, width, tile), BF),
                pltpu.VMEM((2, hz, 1, width, tile), BF),
                pltpu.VMEM((2, width, tile), F32),
                pltpu.VMEM((ncols, rx + 8, width), F32),
                pltpu.VMEM((ncols, rx + 8, width), F32),
                pltpu.VMEM((NY, ry + 8, width), F32),
                pltpu.VMEM((NY, ry + 8, width), F32),
                pltpu.VMEM((NK, rk + 8, width), F32),
                pltpu.VMEM((NK, rk + 8, width), F32),
                pltpu.VMEM((nz, rk + 8, width), F32),
                pltpu.VMEM((ncols, NY, NK, rk, width), F32),
                pltpu.SemaphoreType.DMA((N_MSGS,)),
                pltpu.SemaphoreType.DMA((N_MSGS,)),
                pltpu.SemaphoreType.DMA((nz,)),
            ],
            compiler_params=pltpu.CompilerParams(
                collective_id=0, has_side_effects=True, vmem_limit_bytes=VMEM_LIMIT),
        )(features, weight, bias.reshape(1, width), tiles, src_ids, dst_ids, counts, cotangent)

        per_step = 4

        def back(*refs):
            backward_kernel(dims, per_step, *refs)

        part = pl.pallas_call(
            back,
            name="graph_back",
            grid=(owners // per_step,),
            out_shape=jax.ShapeDtypeStruct((2 * ncols, tile, width), BF),
            in_specs=[smem, smem, smem,
                      pl.BlockSpec((per_step, cap, tile, tile), lambda i: (i, 0, 0, 0)),
                      pl.BlockSpec((2 * nrows, tile, width), lambda i: (0, 0, 0), pipeline_mode=pl.Buffered(1))],
            out_specs=pl.BlockSpec((2 * ncols, tile, width), lambda i: (0, 0, 0)),
            scratch_shapes=[pltpu.VMEM((2 * ncols, tile, width), F32)],
            compiler_params=pltpu.CompilerParams(vmem_limit_bytes=40 * 1024 * 1024),
        )(src_ids, dst_ids, counts, tiles, ga)

        def spread(*refs):
            spread_kernel(ncols, *refs)

        input_grad = pl.pallas_call(
            spread,
            name="graph_spread",
            out_shape=jax.ShapeDtypeStruct((nodes, width), BF),
            in_specs=[vmem, vmem],
            out_specs=vmem,
            scratch_shapes=[
                pltpu.VMEM((ncols - 1, nodes, width), BF),
                pltpu.SemaphoreType.DMA((ncols - 1,)),
                pltpu.SemaphoreType.DMA((ncols - 1,)),
            ],
            compiler_params=pltpu.CompilerParams(collective_id=1, has_side_effects=True),
        )(part.reshape(ncols, nodes, width), weight)
        return out, input_grad, wg, bg.reshape(width)

    in_specs = (
        P(("rows", "cols"), None),
        P(),
        P(),
        P("rows", "cols", None, None, None, None),
        P("rows", "cols", None, None),
        P("rows", "cols", None, None),
        P("rows", "cols", None),
        P(("rows", "cols"), None),
    )
    out_specs = (P(("rows", "cols"), None), P(("rows", "cols"), None), P(), P())
    return jax.shard_map(local, mesh=mesh, in_specs=in_specs, out_specs=out_specs, check_vma=False)
```

```python
import math

import jax
import jax.numpy as jnp
from jax import lax
from jax.experimental import pallas as pl
from jax.experimental.pallas import tpu as pltpu
from jax.sharding import PartitionSpec as P

MESH = pl.DeviceIdType.MESH
BF = jnp.bfloat16
F32 = jnp.float32
NK = 2
NY = 4
VMEM_LIMIT = 63 * 1024 * 1024

RATE = {"x": 46e3, "y": 46e3, "z": 46e3, "k": 300e3}
DELAY = {"x": 2.4, "y": 1.7, "z": 1.7, "k": 1.0}


class Flow:
    def __init__(self):
        self.events = []
        self.msgs = {}

    def msg(self, name, link, nbytes, src, dst, view, peer, slack=0.0):
        self.msgs[name] = dict(idx=len(self.msgs), link=link, nbytes=nbytes, src=src, dst=dst, view=view,
                               peer=peer, slack=slack)

    def event(self, name, needs, fn=None, sends=(), cost=0.15, late=0):
        self.events.append((name, tuple(needs), fn, tuple(sends), cost, late))

    def order(self):
        done, free, now, out = {}, {}, 0.0, []
        pending = list(self.events)
        while pending:
            best = None
            for pos, ev in enumerate(pending):
                if all(n in done for n in ev[1]):
                    ready = max([now] + [done[n] for n in ev[1]])
                    if best is None or (ready, ev[5], pos) < best:
                        best = (ready, ev[5], pos)
            ready, _, pos = best
            ev = pending.pop(pos)
            now = ready + ev[4]
            done[ev[0]] = now
            for s in ev[3]:
                m = self.msgs[s]
                end = max(now, free.get(m["link"], 0.0)) + m["nbytes"] / RATE[m["link"][0]]
                free[m["link"]] = end
                done[s] = end + DELAY[m["link"][0]] + m["slack"]
            out.append(ev)
        self.done = done
        return out

    def emit(self, send_sem, recv_sem):
        waited = set()

        def copy(m):
            return pltpu.make_async_remote_copy(
                src_ref=m["src"](), dst_ref=m["dst"](), send_sem=send_sem.at[m["idx"]],
                recv_sem=recv_sem.at[m["idx"]], device_id=m["peer"], device_id_type=MESH)

        for name, needs, fn, sends, _, _ in self.order():
            for n in needs:
                if n in self.msgs and n not in waited:
                    waited.add(n)
                    m = self.msgs[n]
                    v = m["view"]()
                    pltpu.make_async_remote_copy(
                        src_ref=v, dst_ref=v, send_sem=send_sem.at[m["idx"]],
                        recv_sem=recv_sem.at[m["idx"]], device_id=m["peer"], device_id_type=MESH).wait_recv()
            if fn is not None:
                fn()
            for s in sends:
                copy(self.msgs[s]).start()
        for n, m in self.msgs.items():
            copy(m).wait_send()


def greet(peers):
    barrier = pltpu.get_barrier_semaphore()
    for peer in peers:
        pl.semaphore_signal(barrier, inc=1, device_id=peer, device_id_type=MESH)
    pl.semaphore_wait(barrier, len(peers))


def mod(v, n):
    return lax.rem(v + 2 * n, n)


def main_kernel(dims, feat, weight, bias, tiles, src_ids, dst_ids, counts, cot,
                out, grad, wg, bg,
                av, xf, xt, psend, precv, own0, own1, r0, r1, s0, s1, qt,
                w1, w1r, w2, w2r, w3, w3r, w4r, wtot, ga, sums, sbuf, srecv, prev, last,
                send_sem, recv_sem, load_sem):
    nz, ncols, tile, width, scale = dims
    cap = av.shape[1]
    r = lax.axis_index("rows")
    c = lax.axis_index("cols")
    k = lax.rem(r, NK)
    y = lax.rem(lax.div(r, NK), NY)
    z = lax.div(r, NK * NY)
    hz, hy = nz // 2, NY // 2
    per_core = nz * NY

    def rid(zz, yy, kk):
        return (zz * NY + yy) * NK + kk

    def zdev(o):
        return (rid(mod(z + o, nz), y, k), c)

    def ydev(o):
        return (rid(z, mod(y + o, NY), k), c)

    def xdev(o):
        return (r, mod(c + o, ncols))

    partner = (rid(z, y, 1 - k), c)

    zord = [hz] + [s * d for d in range(hz - 1, 0, -1) for s in (1, -1)] + [0]
    yord = [hy] + [s * d for d in range(hy - 1, 0, -1) for s in (1, -1)] + [0]

    def load(i):
        zz = mod(z + zord[i], nz)
        blk = pl.ds(zz * NY * NK, NY * NK)
        return pltpu.make_async_copy(tiles.at[blk], av.at[blk], load_sem.at[i])

    for i in range(nz):
        load(i).start()

    greet([zdev(o) for o in range(1, nz)] + [ydev(o) for o in range(1, NY)]
          + [xdev(o) for o in range(1, ncols)] + [partner])

    flow = Flow()

    for o in range(1, ncols):
        flow.msg(f"ax{o}", "x", tile * 2 * width * 2 * 1.33,
                 lambda: feat, lambda: xf.at[c], lambda o=o: xf.at[mod(c - o, ncols)], xdev(o))

    def keep_own():
        xf[c] = feat[...]

    flow.event("ax", (), keep_own, [f"ax{o}" for o in range(1, ncols)])

    def turn(o):
        j = mod(c - o, ncols)
        for h in range(2):
            xt[2 * j + h] = xf[j, h * tile:(h + 1) * tile, :].T

    for o in range(ncols):
        flow.event(f"xt{o}", [f"ax{o}" if o else "ax"], lambda o=o: turn(o), cost=0.3)
    flow.event("xt", [f"xt{o}" for o in range(ncols)], cost=0.0)

    def partial_tile(o):
        lhs, rhs = [], []
        cnt = counts[o]
        for s in range(cap):
            t = dst_ids[s, o]
            live = jnp.where(s < cnt, 1, 0)
            m1 = (live * t).astype(F32)
            m0 = (live * (1 - t)).astype(F32)
            a = av[o, s]
            lhs.append(xt[src_ids[s, o]])
            rhs.append(jnp.concatenate(
                [a * jnp.full((tile, tile), m0, F32).astype(BF),
                 a * jnp.full((tile, tile), m1, F32).astype(BF)], axis=1))
        return jnp.dot(jnp.concatenate(lhs, axis=1), jnp.concatenate(rhs, axis=0),
                       preferred_element_type=F32).astype(BF)

    def forward(i):
        zz = mod(z + zord[i], nz)
        load(i).wait()

        def body(jj, carry):
            for u in range(2):
                j = 2 * jj + u
                theirs = partial_tile(rid(zz, j, 1 - k))
                psend[zz, j, 0] = theirs[:, :tile]
                psend[zz, j, 1] = theirs[:, tile:]
            for u in range(2):
                j = 2 * jj + u
                mine = partial_tile(rid(zz, j, k))
                own0[zz, j] = mine[:, :tile]
                own1[j, zz] = mine[:, tile:]
            return carry

        lax.fori_loop(0, NY // 2, body, 0)

    for i in range(nz):
        zat = lambda i=i: mod(z + zord[i], nz)
        flow.msg(f"pe{i}", "k", NY * 2 * width * tile * 2,
                 lambda f=zat: psend.at[f()], lambda f=zat: precv.at[f()], lambda f=zat: precv.at[f()], partner)
        flow.event(f"fw{i}", ["xt"] + ([f"fw{i - 1}"] if i else []), lambda i=i: forward(i), [f"pe{i}"], cost=1.6, late=1)

    halves = {1: pl.ds(0, width // 2), -1: pl.ds(width // 2, width // 2)}

    def chain(tag, n, link, dev, items, buf, extra, rbuf, ready, final):
        h = n // 2
        piece = width * tile * 2

        def rview(i, d, q, rows=None):
            v = rbuf.at[0 if d > 0 else 1, i, q]
            return v if rows is None else v.at[rows]

        def combine(off, it, recvs):
            for d in (1, -1):
                rows = halves[d]
                v = buf(off, it)[rows, :].astype(F32)
                e = extra(off, it) if extra is not None else None
                if e is not None:
                    v = v + e[rows, :].astype(F32)
                for (i, rd, q) in recvs:
                    if i > 0 or rd == d:
                        v = v + rview(i, rd, q)[rows, :].astype(F32)
                yield rows, v

        def store(off, it, recvs):
            dst = buf(off, it)
            for rows, v in combine(off, it, recvs):
                dst[rows, :] = v.astype(BF)

        for q, it in enumerate(items):
            for i in range(h):
                for d in (1, -1):
                    off = d * (h - i)
                    rows = halves[d] if i == 0 else None

                    def src(off=off, it=it, rows=rows):
                        v = buf(off, it)
                        return v if rows is None else v.at[rows]

                    def dst(i=i, d=d, q=q, rows=rows):
                        return rview(i, d, q, rows)

                    flow.msg(f"{tag}.{i}.{d}.{q}", link + ("+" if d > 0 else "-"),
                             piece // 2 if i == 0 else piece, src, dst, dst, dev(d))
            if extra is not None:
                flow.event(f"{tag}.s0.{q}", ready(h, it), lambda it=it: store(h, it, ()),
                           [f"{tag}.0.1.{q}", f"{tag}.0.-1.{q}"])
            else:
                flow.event(f"{tag}.s0.{q}", ready(h, it), None, [f"{tag}.0.1.{q}", f"{tag}.0.-1.{q}"], cost=0.02)
            for i in range(1, h):
                for d in (1, -1):
                    off = d * (h - i)
                    flow.event(f"{tag}.s{i}.{d}.{q}", list(ready(off, it)) + [f"{tag}.{i - 1}.{d}.{q}"],
                               lambda off=off, it=it, i=i, d=d, q=q: store(off, it, [(i - 1, d, q)]),
                               [f"{tag}.{i}.{d}.{q}"])

            def finish(it=it, q=q):
                recvs = [(h - 1, 1, q), (h - 1, -1, q)]
                if final is None:
                    store(0, it, recvs)
                else:
                    for rows, v in combine(0, it, recvs):
                        final[rows, :] = v

            flow.event(f"{tag}.fin.{q}", list(ready(0, it)) + [f"{tag}.{h - 1}.1.{q}", f"{tag}.{h - 1}.-1.{q}"], finish)

    def zpos(off):
        return [i for i, v in enumerate(zord) if (v - off) % nz == 0][0]

    def ypos(off):
        return [i for i, v in enumerate(yord) if (v - off) % NY == 0][0]

    chain("a1", nz, "z", zdev, yord,
          lambda off, dy: own0.at[mod(z + off, nz), mod(y + dy, NY)],
          lambda off, dy: precv.at[mod(z + off, nz), mod(y + dy, NY), 0],
          r0, lambda off, dy: [f"fw{zpos(off)}", f"pe{zpos(off)}"], None)
    chain("b1", NY, "y", ydev, zord,
          lambda off, dz: own1.at[mod(y + off, NY), mod(z + dz, nz)],
          lambda off, dz: precv.at[mod(z + dz, nz), mod(y + off, NY), 1],
          r1, lambda off, dz: [f"fw{zpos(dz)}", f"pe{zpos(dz)}"], None)
    chain("b2", nz, "z", zdev, [0],
          lambda off, it: own1.at[y, mod(z + off, nz)],
          None, s1, lambda off, it: [f"b1.fin.{zpos(off)}"], qt.at[1])
    chain("a2", NY, "y", ydev, [0],
          lambda off, it: own0.at[z, mod(y + off, NY)],
          None, s0, lambda off, it: [f"a1.fin.{ypos(off)}"], qt.at[0])

    slot0 = lambda kk, zz, yy: kk * per_core + zz * NY + yy
    slot1 = lambda kk, zz, yy: (NK + kk) * per_core + yy * nz + zz

    def activate():
        wb = weight[...]
        q = jnp.concatenate([qt[0], qt[1]], axis=1)
        qh = q.astype(BF)
        ql = (q - qh.astype(F32)).astype(BF)
        dn = (((0,), (0,)), ((), ()))
        pre = (lax.dot_general(qh, wb, dn, preferred_element_type=F32)
               + lax.dot_general(ql, wb, dn, preferred_element_type=F32) + bias[...])
        ks = math.sqrt(2.0 / math.pi)
        sq = pre * pre
        th = jnp.tanh(ks * pre * (1.0 + 0.044715 * sq))
        out[...] = (0.5 * pre * (1.0 + th)).astype(BF)
        slope = 0.5 * (1.0 + th) + 0.5 * pre * (1.0 - th * th) * (ks * (1.0 + 3 * 0.044715 * sq))
        g = (cot[...].astype(F32) * slope).astype(BF)
        ga[slot0(k, z, y)] = g[:tile]
        ga[slot1(k, z, y)] = g[tile:]

    flow.event("act", ["a2.fin.0", "b2.fin.0"], activate, cost=1.5)

    ghalf = {1: pl.ds(0, tile // 2), -1: pl.ds(tile // 2, tile // 2)}

    def gather(tag, n, link, dev, items, slot, ready):
        h = n // 2
        piece = tile * width * 2

        def view(off, it, rows):
            v = ga.at[slot(off, it)]
            return v if rows is None else v.at[rows]

        for q, it in enumerate(items):
            for i in range(h):
                for d in (1, -1):
                    rows = ghalf[d] if i == h - 1 else None
                    flow.msg(f"{tag}.{i}.{d}.{q}", link + ("+" if d > 0 else "-"),
                             piece // 2 if i == h - 1 else piece,
                             lambda i=i, d=d, it=it, rows=rows: view(-i * d, it, rows),
                             lambda i=i, d=d, it=it, rows=rows: view(-i * d, it, rows),
                             lambda i=i, d=d, it=it, rows=rows: view(-(i + 1) * d, it, rows), dev(d))
            flow.event(f"{tag}.s.{q}", ready(it), None, [f"{tag}.0.1.{q}", f"{tag}.0.-1.{q}"], cost=0.02)
            for i in range(h - 1):
                for d in (1, -1):
                    flow.event(f"{tag}.f{i}.{d}.{q}", [f"{tag}.{i}.{d}.{q}"], None, [f"{tag}.{i + 1}.{d}.{q}"], cost=0.02)
            flow.event(f"{tag}.last.{q}", [f"{tag}.{h - 1}.1.{q}", f"{tag}.{h - 1}.-1.{q}"], None, cost=0.02)

        def have(off, q, own):
            off = off % n
            if off == 0:
                return own
            if off == h:
                return f"{tag}.last.{q}"
            return f"{tag}.f{off - 1}.-1.{q}" if off < h else f"{tag}.f{n - off - 1}.1.{q}"

        return have

    have_a1 = gather("ga1", NY, "y", ydev, [0],
                     lambda off, it: slot0(k, z, mod(y + off, NY)), lambda it: ["act"])
    have_b1 = gather("gb1", nz, "z", zdev, [0],
                     lambda off, it: slot1(k, mod(z + off, nz), y), lambda it: ["act"])
    near_y, near_z = yord[::-1], zord[::-1]
    have_a2 = gather("ga2", nz, "z", zdev, near_y,
                     lambda off, dy: slot0(k, mod(z + off, nz), mod(y + dy, NY)),
                     lambda dy: [have_a1(dy, 0, "act")])
    have_b2 = gather("gb2", NY, "y", ydev, near_z,
                     lambda off, dz: slot1(k, mod(z + dz, nz), mod(y + off, NY)),
                     lambda dz: [have_b1(dz, 0, "act")])
    ready0, ready1 = {}, {}
    for q, dy in enumerate(near_y):
        for dz in near_z:
            have = have_a2(dz, q, have_a1(dy, 0, "act"))
            mine = lambda dz=dz, dy=dy: ga.at[slot0(k, mod(z + dz, nz), mod(y + dy, NY))]
            other = lambda dz=dz, dy=dy: ga.at[slot0(1 - k, mod(z + dz, nz), mod(y + dy, NY))]
            flow.msg(f"ka{dz}.{dy}", "k", tile * width * 2, mine, mine, other, partner)
            flow.event(f"kas{dz}.{dy}", [have], None, [f"ka{dz}.{dy}"], cost=0.02)
            ready0[dz, dy] = (have, f"ka{dz}.{dy}")
    for q, dz in enumerate(near_z):
        for dy in near_y:
            have = have_b2(dy, q, have_b1(dz, 0, "act"))
            mine = lambda dz=dz, dy=dy: ga.at[slot1(k, mod(z + dz, nz), mod(y + dy, NY))]
            other = lambda dz=dz, dy=dy: ga.at[slot1(1 - k, mod(z + dz, nz), mod(y + dy, NY))]
            flow.msg(f"kb{dz}.{dy}", "k", tile * width * 2, mine, mine, other, partner)
            flow.event(f"kbs{dz}.{dy}", [have], None, [f"kb{dz}.{dy}"], cost=0.02)
            ready1[dz, dy] = (have, f"kb{dz}.{dy}")

    rx, ry, rk = width // ncols, width // ncols // NY, width // ncols // NY // NK

    def wpart():
        q = jnp.concatenate([qt[0], qt[1]], axis=1).astype(BF)
        g = jnp.concatenate([ga[slot0(k, z, y)], ga[slot1(k, z, y)]], axis=0)
        w = jnp.dot(q, g, preferred_element_type=F32)
        b = jnp.broadcast_to(jnp.sum(g.astype(F32), axis=0, keepdims=True), (8, width))
        for j in range(ncols):
            w1[j, :rx] = w[j * rx:(j + 1) * rx]
            w1[j, rx:] = b
        w1r[c] = w1[c]

    for o in range(1, ncols):
        flow.msg(f"w1.{o}", "x", (rx + 8) * width * 4,
                 lambda o=o: w1.at[mod(c + o, ncols)], lambda: w1r.at[c], lambda o=o: w1r.at[mod(c - o, ncols)], xdev(o), slack=2.0)
    flow.event("w1", ["act", "ga1.s.0", "gb1.s.0"], wpart, [f"w1.{o}" for o in range(1, ncols)], cost=0.8)

    def wsum2():
        t = w1r[0]
        for j in range(1, ncols):
            t = t + w1r[j]
        for j in range(NY):
            w2[j, :ry] = t[j * ry:(j + 1) * ry]
            w2[j, ry:] = t[rx:]
        w2r[y] = w2[y]

    for o in range(1, NY):
        flow.msg(f"w2.{o}", "y+", (ry + 8) * width * 4,
                 lambda o=o: w2.at[mod(y + o, NY)], lambda: w2r.at[y], lambda o=o: w2r.at[mod(y - o, NY)], ydev(o), slack=2.0)
    flow.event("w2", ["w1"] + [f"w1.{o}" for o in range(1, ncols)], wsum2, [f"w2.{o}" for o in range(1, NY)])

    def wsum3():
        t = w2r[0]
        for j in range(1, NY):
            t = t + w2r[j]
        for j in range(NK):
            w3[j, :rk] = t[j * rk:(j + 1) * rk]
            w3[j, rk:] = t[ry:]
        w3r[k] = w3[k]

    flow.msg("w3", "k", (rk + 8) * width * 4, lambda: w3.at[1 - k], lambda: w3r.at[k], lambda: w3r.at[1 - k], partner)
    flow.event("w3s", ["w2"] + [f"w2.{o}" for o in range(1, NY)], wsum3, ["w3"])

    def wsum4():
        w4r[z] = w3r[0] + w3r[1]

    for o in range(1, nz):
        flow.msg(f"w4.{o}", "z+", (rk + 8) * width * 4,
                 lambda: w4r.at[z], lambda: w4r.at[z], lambda o=o: w4r.at[mod(z - o, nz)], zdev(o), slack=4.0)
    flow.event("w4s", ["w3s", "w3"], wsum4, [f"w4.{o}" for o in range(1, nz)])

    def wsum5():
        t = w4r[0]
        for j in range(1, nz):
            t = t + w4r[j]
        t = t * scale
        wtot[c, y, k] = t[:rk]
        bg[...] = t[rk:rk + 1]

    flow.msg("w5", "k", rk * width * 4, lambda: wtot.at[c, y, k], lambda: wtot.at[c, y, k],
             lambda: wtot.at[c, y, 1 - k], partner)
    flow.event("w5s", ["w4s"] + [f"w4.{o}" for o in range(1, nz)], wsum5, ["w5"])
    for o in range(1, NY):
        flow.msg(f"w6.{o}", "y+", ry * width * 4, lambda: wtot.at[c, y], lambda: wtot.at[c, y],
                 lambda o=o: wtot.at[c, mod(y - o, NY)], ydev(o), slack=2.0)
    flow.event("w6s", ["w5s", "w5"], None, [f"w6.{o}" for o in range(1, NY)])
    for o in range(1, ncols):
        flow.msg(f"w7.{o}", "x", rx * width * 4, lambda: wtot.at[c], lambda: wtot.at[c],
                 lambda o=o: wtot.at[mod(c - o, ncols)], xdev(o), slack=2.0)
    flow.event("w7s", ["w6s"] + [f"w6.{o}" for o in range(1, NY)], None, [f"w7.{o}" for o in range(1, ncols)])

    def wend():
        for a in range(ncols):
            for b in range(NY):
                for e in range(NK):
                    base = a * rx + b * ry + e * rk
                    wg[base:base + rk] = wtot[a, b, e]

    flow.event("wend", ["w7s"] + [f"w7.{o}" for o in range(1, ncols)], wend)
    flow.order()
    when = flow.done
    seq = sorted((max(when[ready0[dz, dy][side]], when[ready1[dz, dy][side]]), side, dz, dy)
                 for side in range(2) for dz in near_z for dy in near_y)
    seq = [(side, dz, dy) for _, side, dz, dy in seq]
    n_slots = len(seq) * cap
    n_src = 2 * ncols

    def owner(n):
        side, dz, dy = seq[n]
        return mod(z + dz, nz), mod(y + dy, NY), (1 - k if side else k)

    def links():
        ends = [jnp.int32(n_slots)] * n_src
        for n in range(len(seq)):
            o = rid(*owner(n))
            cnt = counts[o]
            for s in range(cap):
                src = src_ids[s, o]
                live = s < cnt
                p = ends[0]
                for j in range(1, n_src):
                    p = jnp.where(src == j, ends[j], p)
                prev[n * cap + s] = p
                for j in range(n_src):
                    ends[j] = jnp.where(jnp.logical_and(src == j, live), n * cap + s, ends[j])
        for j in range(n_src):
            last[j] = ends[j]
        sums[n_slots] = jnp.zeros((tile, width), F32)

    flow.event("links", ["ax"], links, cost=1.5)

    def backward(n0, n1):
        terms = []
        for n in range(n0, n1):
            zz, yy, kk = owner(n)
            o = rid(zz, yy, kk)
            g0 = ga[slot0(kk, zz, yy)]
            g1 = ga[slot1(kk, zz, yy)]
            for s in range(cap):
                g = jnp.where(dst_ids[s, o] == 0, g0, g1)
                terms.append(jnp.dot(av[o, s], g, preferred_element_type=F32))
        for i, t in enumerate(terms):
            i = n0 * cap + i
            sums[i] = t + sums[prev[i]]

    group = 2
    for n0 in range(0, len(seq), group):
        needs = ["links", "fw7"] + ([f"bw{n0 - group}"] if n0 else [])
        for n in range(n0, n0 + group):
            side, dz, dy = seq[n]
            needs += [ready0[dz, dy][side], ready1[dz, dy][side]]
        flow.event(f"bw{n0}", needs, lambda n0=n0: backward(n0, n0 + group), cost=0.35, late=1)
    bw_end = f"bw{len(seq) - group}"

    def give(o):
        j = mod(c + o, ncols)
        for h in range(2):
            sbuf[j, h * tile:(h + 1) * tile, :] = sums[last[2 * j + h]].astype(BF)

    for o in (2, 1, 3):
        flow.msg(f"sp{o}", "x", 2 * tile * width * 2,
                 lambda o=o: sbuf.at[mod(c + o, ncols)], lambda: srecv.at[c], lambda o=o: srecv.at[mod(c - o, ncols)], xdev(o))
        flow.event(f"sps{o}", [bw_end], lambda o=o: give(o), [f"sp{o}"])

    def settle():
        for h in range(2):
            rows = slice(h * tile, (h + 1) * tile)
            t = sums[last[2 * c + h]]
            for o in range(1, ncols):
                t = t + srecv[mod(c - o, ncols), rows, :].astype(F32)
            grad[rows, :] = t.astype(BF)

    flow.event("settle", [f"sps{o}" for o in range(1, ncols)] + [f"sp{o}" for o in range(1, ncols)], settle)
    flow.emit(send_sem, recv_sem)


N_MSGS = 256


def end_kernel(out, grad, wg, bg, weight, out_o, input_o, wg_o, bg_o):
    out_o[...] = out[...]
    input_o[...] = lax.dot_general(
        grad[...], weight[...], (((1,), (1,)), ((), ())), preferred_element_type=F32).astype(BF)
    wg_o[...] = wg[...]
    bg_o[...] = bg[...]


def solution(mesh):
    nrows, ncols = mesh.shape["rows"], mesh.shape["cols"]
    nz = nrows // (NK * NY)
    vmem = pl.BlockSpec(memory_space=pltpu.VMEM)
    smem = pl.BlockSpec(memory_space=pltpu.SMEM)
    anym = pl.BlockSpec(memory_space=pl.ANY)

    def local(features, weight, bias, tile_values, tile_source, tile_dest, send_counts, cotangent):
        owners, cap, tile = tile_values.shape[2:5]
        nodes, width = features.shape
        scale = 1.0 / math.sqrt(nodes * nrows * ncols)
        dims = (nz, ncols, tile, width, scale)
        tiles = tile_values.reshape(owners, cap, tile, tile)
        src_ids = jnp.transpose(tile_source, (0, 3, 1, 2)).reshape(cap, owners)
        dst_ids = jnp.transpose(tile_dest, (0, 3, 1, 2)).reshape(cap, owners)
        counts = send_counts.reshape(owners)
        rx = width // ncols
        ry, rk = rx // NY, rx // NY // NK
        hz, hy = nz // 2, NY // 2

        def body(*refs):
            main_kernel(dims, *refs)

        out, grad, wg, bg = pl.pallas_call(
            body,
            name="graph_main",
            out_shape=(
                jax.ShapeDtypeStruct((nodes, width), BF),
                jax.ShapeDtypeStruct((nodes, width), BF),
                jax.ShapeDtypeStruct((width, width), F32),
                jax.ShapeDtypeStruct((1, width), F32),
            ),
            in_specs=[vmem, vmem, vmem, anym, smem, smem, smem, vmem],
            out_specs=(vmem, vmem, vmem, vmem),
            scratch_shapes=[
                pltpu.VMEM((owners, cap, tile, tile), BF),
                pltpu.VMEM((ncols, nodes, width), BF),
                pltpu.VMEM((2 * ncols, width, tile), BF),
                pltpu.VMEM((nz, NY, 2, width, tile), BF),
                pltpu.VMEM((nz, NY, 2, width, tile), BF),
                pltpu.VMEM((nz, NY, width, tile), BF),
                pltpu.VMEM((NY, nz, width, tile), BF),
                pltpu.VMEM((2, hz, NY, width, tile), BF),
                pltpu.VMEM((2, hy, nz, width, tile), BF),
                pltpu.VMEM((2, hy, 1, width, tile), BF),
                pltpu.VMEM((2, hz, 1, width, tile), BF),
                pltpu.VMEM((2, width, tile), F32),
                pltpu.VMEM((ncols, rx + 8, width), F32),
                pltpu.VMEM((ncols, rx + 8, width), F32),
                pltpu.VMEM((NY, ry + 8, width), F32),
                pltpu.VMEM((NY, ry + 8, width), F32),
                pltpu.VMEM((NK, rk + 8, width), F32),
                pltpu.VMEM((NK, rk + 8, width), F32),
                pltpu.VMEM((nz, rk + 8, width), F32),
                pltpu.VMEM((ncols, NY, NK, rk, width), F32),
                pltpu.VMEM((2 * nrows, tile, width), BF),
                pltpu.VMEM((owners * cap + 1, tile, width), F32),
                pltpu.VMEM((ncols, nodes, width), BF),
                pltpu.VMEM((ncols, nodes, width), BF),
                pltpu.SMEM((owners * cap,), jnp.int32),
                pltpu.SMEM((2 * ncols,), jnp.int32),
                pltpu.SemaphoreType.DMA((N_MSGS,)),
                pltpu.SemaphoreType.DMA((N_MSGS,)),
                pltpu.SemaphoreType.DMA((nz,)),
            ],
            compiler_params=pltpu.CompilerParams(
                collective_id=0, has_side_effects=True, vmem_limit_bytes=VMEM_LIMIT),
        )(features, weight, bias.reshape(1, width), tiles, src_ids, dst_ids, counts, cotangent)

        out, input_grad, wg, bg = pl.pallas_call(
            end_kernel,
            name="graph_end",
            out_shape=(
                jax.ShapeDtypeStruct((nodes, width), BF),
                jax.ShapeDtypeStruct((nodes, width), BF),
                jax.ShapeDtypeStruct((width, width), F32),
                jax.ShapeDtypeStruct((1, width), F32),
            ),
            in_specs=[vmem] * 5,
            out_specs=(vmem,) * 4,
        )(out, grad, wg, bg, weight)
        return out, input_grad, wg, bg.reshape(width)

    in_specs = (
        P(("rows", "cols"), None),
        P(),
        P(),
        P("rows", "cols", None, None, None, None),
        P("rows", "cols", None, None),
        P("rows", "cols", None, None),
        P("rows", "cols", None),
        P(("rows", "cols"), None),
    )
    out_specs = (P(("rows", "cols"), None), P(("rows", "cols"), None), P(), P())
    return jax.shard_map(local, mesh=mesh, in_specs=in_specs, out_specs=out_specs, check_vma=False)
```

```python
import math

import jax
import jax.numpy as jnp
from jax import lax
from jax.experimental import pallas as pl
from jax.experimental.pallas import tpu as pltpu
from jax.sharding import PartitionSpec as P

MESH = pl.DeviceIdType.MESH
BF = jnp.bfloat16
F32 = jnp.float32
NK = 2
NY = 4
VMEM_LIMIT = 63 * 1024 * 1024

RATE = {"x": 46e3, "y": 46e3, "z": 46e3, "k": 400e3}
BACKLOG = 0.4
DELAY = {"x": 2.4, "y": 1.7, "z": 1.7, "k": 1.0}


class Flow:
    def __init__(self):
        self.events = []
        self.msgs = {}

    def msg(self, name, link, nbytes, src, dst, view, peer, slack=0.0):
        self.msgs[name] = dict(idx=len(self.msgs), link=link, nbytes=nbytes, src=src, dst=dst, view=view,
                               peer=peer, slack=slack)

    def event(self, name, needs, fn=None, sends=(), cost=0.15, late=0):
        self.events.append((name, tuple(needs), fn, tuple(sends), cost, late))

    def order(self):
        done, free, now, out = {}, {}, 0.0, []
        pending = list(self.events)
        while pending:
            best = None
            for pos, ev in enumerate(pending):
                if all(n in done for n in ev[1]):
                    ready = max([now] + [done[n] for n in ev[1]]
                                + [free.get(self.msgs[m]["link"], 0.0) - BACKLOG for m in ev[3] if ev[5] > -50 and self.msgs[m]["link"] != "k"])
                    if best is None or (ready, ev[5], pos) < best:
                        best = (ready, ev[5], pos)
            ready, _, pos = best
            ev = pending.pop(pos)
            now = ready + ev[4]
            done[ev[0]] = now
            for s in ev[3]:
                m = self.msgs[s]
                end = max(now, free.get(m["link"], 0.0)) + m["nbytes"] / RATE[m["link"][0]]
                free[m["link"]] = end
                done[s] = end + DELAY[m["link"][0]] + m["slack"]
            out.append(ev)
        self.done = done
        return out

    def emit(self, send_sem, recv_sem):
        waited = set()

        def copy(m):
            return pltpu.make_async_remote_copy(
                src_ref=m["src"](), dst_ref=m["dst"](), send_sem=send_sem.at[m["idx"]],
                recv_sem=recv_sem.at[m["idx"]], device_id=m["peer"], device_id_type=MESH)

        for name, needs, fn, sends, _, _ in self.order():
            for n in needs:
                if n in self.msgs and n not in waited:
                    waited.add(n)
                    m = self.msgs[n]
                    v = m["view"]()
                    pltpu.make_async_remote_copy(
                        src_ref=v, dst_ref=v, send_sem=send_sem.at[m["idx"]],
                        recv_sem=recv_sem.at[m["idx"]], device_id=m["peer"], device_id_type=MESH).wait_recv()
            if fn is not None:
                fn()
            for s in sends:
                copy(self.msgs[s]).start()
        for n, m in self.msgs.items():
            copy(m).wait_send()


def greet(peers):
    barrier = pltpu.get_barrier_semaphore()
    for peer in peers:
        pl.semaphore_signal(barrier, inc=1, device_id=peer, device_id_type=MESH)
    pl.semaphore_wait(barrier, len(peers))


def mod(v, n):
    return lax.rem(v + 2 * n, n)


def main_kernel(dims, feat, weight, bias, tiles, src_ids, dst_ids, counts, cot,
                out, grad, wg, bg,
                av, xf, xt, psend, precv, own0, own1, r0, r1, s0, s1, qt,
                w1, w1r, w2, w2r, w3, w3r, w4r, wtot, ga, sums, sbuf, srecv, prev, last,
                send_sem, recv_sem, load_sem):
    nz, ncols, tile, width, scale = dims
    cap = av.shape[1]
    r = lax.axis_index("rows")
    c = lax.axis_index("cols")
    k = lax.rem(r, NK)
    y = lax.rem(lax.div(r, NK), NY)
    z = lax.div(r, NK * NY)
    hz, hy = nz // 2, NY // 2
    per_core = nz * NY

    def rid(zz, yy, kk):
        return (zz * NY + yy) * NK + kk

    def zdev(o):
        return (rid(mod(z + o, nz), y, k), c)

    def ydev(o):
        return (rid(z, mod(y + o, NY), k), c)

    def xdev(o):
        return (r, mod(c + o, ncols))

    partner = (rid(z, y, 1 - k), c)

    zord = [hz] + [s * d for d in range(hz - 1, 0, -1) for s in (1, -1)] + [0]
    yord = [hy] + [s * d for d in range(hy - 1, 0, -1) for s in (1, -1)] + [0]

    def load(i):
        zz = mod(z + zord[i], nz)
        blk = pl.ds(zz * NY * NK, NY * NK)
        return pltpu.make_async_copy(tiles.at[blk], av.at[blk], load_sem.at[i])

    for i in range(nz):
        load(i).start()

    greet([zdev(o) for o in range(1, nz)] + [ydev(o) for o in range(1, NY)]
          + [xdev(o) for o in range(1, ncols)] + [partner])

    flow = Flow()

    def gather(tag, n, link, dev, items, rows, view, ready, own=None, prio=4):
        h = n // 2
        piece = rows * width * 2
        part = {1: pl.ds(0, rows // 2), -1: pl.ds(rows // 2, rows // 2)}

        def cut(ref, d, i):
            return ref.at[part[d]] if i == h - 1 else ref

        for q, it in enumerate(items):
            for i in range(h):
                for d in (1, -1):
                    def src(i=i, d=d, it=it):
                        ref = own(it) if own is not None and i == 0 else view(-i * d, it)
                        return cut(ref, d, i)

                    flow.msg(f"{tag}.{i}.{d}.{q}", link + ("+" if d > 0 else "-"),
                             piece // 2 if i == h - 1 else piece, src,
                             lambda i=i, d=d, it=it: cut(view(-i * d, it), d, i),
                             lambda i=i, d=d, it=it: cut(view(-(i + 1) * d, it), d, i), dev(d))
            flow.event(f"{tag}.s.{q}", ready(it), None, [f"{tag}.0.1.{q}", f"{tag}.0.-1.{q}"], cost=0.02, late=prio)
            for i in range(h - 1):
                for d in (1, -1):
                    flow.event(f"{tag}.f{i}.{d}.{q}", [f"{tag}.{i}.{d}.{q}"], None, [f"{tag}.{i + 1}.{d}.{q}"], cost=0.02, late=prio + i + 1)
            flow.event(f"{tag}.last.{q}", [f"{tag}.{h - 1}.1.{q}", f"{tag}.{h - 1}.-1.{q}"], None, cost=0.02)

        def have(off, q, mine):
            off = off % n
            if off == 0:
                return mine
            if off == h:
                return f"{tag}.last.{q}"
            return f"{tag}.f{off - 1}.-1.{q}" if off < h else f"{tag}.f{n - off - 1}.1.{q}"

        return have

    def xrows(it):
        return pl.ds(it * tile, tile)

    have_x = gather("ax", ncols, "x", xdev, [0, 1], tile,
                    lambda off, it: xf.at[mod(c + off, ncols), xrows(it)], lambda it: [],
                    lambda it: feat.at[xrows(it)])
    xts = []
    for off in [0, 1, -1, ncols // 2]:
        for h in range(2):
            def turn(off=off, h=h):
                block = feat[h * tile:(h + 1) * tile, :] if off == 0 else xf[mod(c + off, ncols), h * tile:(h + 1) * tile, :]
                xt[2 * mod(c + off, ncols) + h] = block.T

            flow.event(f"xt{off}.{h}", [have_x(off, h, f"ax.s.{h}"), "ax.s.1"], turn, cost=0.2, late=5)
            xts.append(f"xt{off}.{h}")
    flow.event("xt", xts, cost=0.0)

    cut_f = (width * 3) // 8
    def partial_tile(o):
        lhs, rhs = [], []
        cnt = counts[o]
        for s in range(cap):
            t = dst_ids[s, o]
            live = jnp.where(s < cnt, 1, 0)
            m1 = (live * t).astype(F32)
            m0 = (live * (1 - t)).astype(F32)
            a = av[o, s]
            lhs.append(xt[src_ids[s, o]])
            rhs.append(jnp.concatenate(
                [a * jnp.full((tile, tile), m0, F32).astype(BF),
                 a * jnp.full((tile, tile), m1, F32).astype(BF)], axis=1))
        return jnp.dot(jnp.concatenate(lhs, axis=1), jnp.concatenate(rhs, axis=0),
                       preferred_element_type=F32).astype(BF)

    def forward(i, side):
        zz = mod(z + zord[i], nz)
        if side:
            load(i).wait()

        def body(jj, carry):
            for u in range(2):
                j = 2 * jj + u
                if side:
                    psend[zz, j] = partial_tile(rid(zz, j, 1 - k))
                else:
                    mine = partial_tile(rid(zz, j, k))
                    own0[zz, j] = mine[:cut_f]
                    own1[j, zz] = mine[cut_f:]
            return carry

        lax.fori_loop(0, NY // 2, body, 0)

    for i in range(nz):
        zat = lambda i=i: mod(z + zord[i], nz)
        flow.msg(f"pe{i}", "k", NY * 2 * width * tile * 2,
                 lambda f=zat: psend.at[f()], lambda f=zat: precv.at[f()], lambda f=zat: precv.at[f()], partner)
        flow.event(f"ft{i}", ["xt"] + ([f"fw{i - 1}"] if i else []), lambda i=i: forward(i, True), [f"pe{i}"], cost=0.65, late=20)
        flow.event(f"fw{i}", [f"ft{i}"], lambda i=i: forward(i, False), cost=0.65, late=20)

    def chain(tag, n, link, dev, items, length, buf, extra, rbuf, ready, final, value=None, prio=0, buf_cols=width):
        halves = {1: pl.ds(0, length // 2), -1: pl.ds(length // 2, length // 2)}
        h = n // 2
        piece = length * buf_cols * 2

        def rview(i, d, q, rows=None):
            v = rbuf.at[0 if d > 0 else 1, i, q]
            return v if rows is None else v.at[rows]

        def combine(off, it, recvs):
            for d in (1, -1):
                rows = halves[d]
                v = buf(off, it)[rows, :].astype(F32) if value is None else value(off, it, rows)
                e = extra(off, it) if extra is not None else None
                if e is not None:
                    v = v + e[rows, :].astype(F32)
                for (i, rd, q) in recvs:
                    if i > 0 or rd == d:
                        v = v + rview(i, rd, q)[rows, :].astype(F32)
                yield rows, v

        def store(off, it, recvs):
            dst = buf(off, it)
            for rows, v in combine(off, it, recvs):
                dst[rows, :] = v.astype(BF)

        for q, it in enumerate(items):
            for i in range(h):
                for d in (1, -1):
                    off = d * (h - i)
                    rows = halves[d] if i == 0 else None

                    def src(off=off, it=it, rows=rows):
                        v = buf(off, it)
                        return v if rows is None else v.at[rows]

                    def dst(i=i, d=d, q=q, rows=rows):
                        return rview(i, d, q, rows)

                    flow.msg(f"{tag}.{i}.{d}.{q}", link + ("+" if d > 0 else "-"),
                             piece // 2 if i == 0 else piece, src, dst, dst, dev(d))
            if extra is not None or value is not None:
                flow.event(f"{tag}.s0.{q}", ready(h, it), lambda it=it: store(h, it, ()),
                           [f"{tag}.0.1.{q}", f"{tag}.0.-1.{q}"], late=prio)
            else:
                flow.event(f"{tag}.s0.{q}", ready(h, it), None, [f"{tag}.0.1.{q}", f"{tag}.0.-1.{q}"], cost=0.02)
            for i in range(1, h):
                for d in (1, -1):
                    off = d * (h - i)
                    flow.event(f"{tag}.s{i}.{d}.{q}", list(ready(off, it)) + [f"{tag}.{i - 1}.{d}.{q}"],
                               lambda off=off, it=it, i=i, d=d, q=q: store(off, it, [(i - 1, d, q)]),
                               [f"{tag}.{i}.{d}.{q}"], late=prio + i)

            def finish(it=it, q=q):
                recvs = [(h - 1, 1, q), (h - 1, -1, q)]
                if final is None:
                    store(0, it, recvs)
                else:
                    for rows, v in combine(0, it, recvs):
                        final(it)[rows, :] = v.astype(final(it).dtype)

            flow.event(f"{tag}.fin.{q}", list(ready(0, it)) + [f"{tag}.{h - 1}.1.{q}", f"{tag}.{h - 1}.-1.{q}"], finish, late=prio)

    def zpos(off):
        return [i for i, v in enumerate(zord) if (v - off) % nz == 0][0]

    def ypos(off):
        return [i for i, v in enumerate(yord) if (v - off) % NY == 0][0]

    rows_lo, rows_hi = pl.ds(0, cut_f), pl.ds(cut_f, width - cut_f)
    chain("a1", nz, "z", zdev, yord, cut_f,
          lambda off, dy: own0.at[mod(z + off, nz), mod(y + dy, NY)],
          lambda off, dy: precv.at[mod(z + off, nz), mod(y + dy, NY), rows_lo],
          r0, lambda off, dy: [f"fw{zpos(off)}", f"pe{zpos(off)}"], None, prio=4)
    chain("b1", NY, "y", ydev, zord, width - cut_f,
          lambda off, dz: own1.at[mod(y + off, NY), mod(z + dz, nz)],
          lambda off, dz: precv.at[mod(z + dz, nz), mod(y + off, NY), rows_hi],
          r1, lambda off, dz: [f"fw{zpos(dz)}", f"pe{zpos(dz)}"], None, prio=4)
    chain("b2", nz, "z", zdev, [0], width - cut_f,
          lambda off, it: own1.at[y, mod(z + off, nz)],
          None, s1, lambda off, it: [f"b1.fin.{zpos(off)}"], lambda it: qt.at[rows_hi])
    chain("a2", NY, "y", ydev, [0], cut_f,
          lambda off, it: own0.at[z, mod(y + off, NY)],
          None, s0, lambda off, it: [f"a1.fin.{ypos(off)}"], lambda it: qt.at[rows_lo])

    slot = lambda kk, zz, yy: kk * per_core + zz * NY + yy

    def activate(t):
        rows = slice(t * tile, (t + 1) * tile)
        wb = weight[...]
        q = qt[:, rows]
        qh = q.astype(BF)
        ql = (q - qh.astype(F32)).astype(BF)
        dn = (((0,), (0,)), ((), ()))
        pre = (lax.dot_general(qh, wb, dn, preferred_element_type=F32)
               + lax.dot_general(ql, wb, dn, preferred_element_type=F32) + bias[...])
        ks = math.sqrt(2.0 / math.pi)
        sq = pre * pre
        th = jnp.tanh(ks * pre * (1.0 + 0.044715 * sq))
        slope = 0.5 * (1.0 + th) + 0.5 * pre * (1.0 - th * th) * (ks * (1.0 + 3 * 0.044715 * sq))
        ga[slot(k, z, y), rows, :] = (cot[rows, :].astype(F32) * slope).astype(BF)
        out[rows, :] = (0.5 * pre * (1.0 + th)).astype(BF)

    flow.event("act0", ["a2.fin.0", "b2.fin.0"], lambda: activate(0), cost=0.8)
    flow.event("act1", ["act0"], lambda: activate(1), cost=0.8)
    flow.event("act", ["act0", "act1"], cost=0.0)

    cut_a = (tile * 3) // 4
    rows_a, rows_b = pl.ds(0, cut_a), pl.ds(cut_a, 2 * tile - cut_a)
    len_b = 2 * tile - cut_a

    def gview(kk, dz, dy, rows):
        return ga.at[slot(kk, mod(z + dz, nz), mod(y + dy, NY)), rows]

    have_a1 = gather("ga1", NY, "y", ydev, [0], cut_a,
                     lambda off, it: gview(k, 0, off, rows_a), lambda it: ["act0"], prio=-4)
    have_b1 = gather("gb1", nz, "z", zdev, [0], len_b,
                     lambda off, it: gview(k, off, 0, rows_b), lambda it: ["act"], prio=-8)
    near_y, near_z = yord[::-1], zord[::-1]
    have_a2 = gather("ga2", nz, "z", zdev, near_y, cut_a,
                     lambda off, dy: gview(k, off, dy, rows_a), lambda dy: [have_a1(dy, 0, "act0")])
    have_b2 = gather("gb2", NY, "y", ydev, near_z, len_b,
                     lambda off, dz: gview(k, dz, off, rows_b), lambda dz: [have_b1(dz, 0, "act")])
    ready0, ready1 = {}, {}
    for dz in near_z:
        for dy in near_y:
            have = have_a2(dz, near_y.index(dy), have_a1(dy, 0, "act0"))
            mine = lambda dz=dz, dy=dy: gview(k, dz, dy, rows_a)
            other = lambda dz=dz, dy=dy: gview(1 - k, dz, dy, rows_a)
            flow.msg(f"ka{dz}.{dy}", "k", cut_a * width * 2, mine, mine, other, partner)
            flow.event(f"kas{dz}.{dy}", [have], None, [f"ka{dz}.{dy}"], cost=0.02)
            ready0[dz, dy] = (have, f"ka{dz}.{dy}")
            have = have_b2(dy, near_z.index(dz), have_b1(dz, 0, "act"))
            mine = lambda dz=dz, dy=dy: gview(k, dz, dy, rows_b)
            other = lambda dz=dz, dy=dy: gview(1 - k, dz, dy, rows_b)
            flow.msg(f"kb{dz}.{dy}", "k", len_b * width * 2, mine, mine, other, partner)
            flow.event(f"kbs{dz}.{dy}", [have], None, [f"kb{dz}.{dy}"], cost=0.02)
            ready1[dz, dy] = (have, f"kb{dz}.{dy}")

    rx, ry, rk = width // ncols, width // ncols // NY, width // ncols // NY // NK

    def wpart():
        q = qt[...].astype(BF)
        g = ga[slot(k, z, y)]
        w = jnp.dot(q, g, preferred_element_type=F32)
        b = jnp.broadcast_to(jnp.sum(g.astype(F32), axis=0, keepdims=True), (8, width))
        for j in range(ncols):
            w1[j, :rx] = w[j * rx:(j + 1) * rx]
            w1[j, rx:] = b
        w1r[c] = w1[c]

    for o in range(1, ncols):
        flow.msg(f"w1.{o}", "x", (rx + 8) * width * 4,
                 lambda o=o: w1.at[mod(c + o, ncols)], lambda: w1r.at[c], lambda o=o: w1r.at[mod(c - o, ncols)], xdev(o), slack=0.5)
    flow.event("w1", ["act", "ga1.s.0", "gb1.s.0", "ga2.s.0", "gb2.s.0"], wpart,
               [f"w1.{o}" for o in range(1, ncols)], cost=1.2, late=15)

    def wsum2():
        t = w1r[0]
        for j in range(1, ncols):
            t = t + w1r[j]
        for j in range(NY):
            w2[j, :ry] = t[j * ry:(j + 1) * ry]
            w2[j, ry:] = t[rx:]
        w2r[y] = w2[y]

    for o in range(1, NY):
        flow.msg(f"w2.{o}", "y+", (ry + 8) * width * 4,
                 lambda o=o: w2.at[mod(y + o, NY)], lambda: w2r.at[y], lambda o=o: w2r.at[mod(y - o, NY)], ydev(o), slack=0.5)
    flow.event("w2", ["w1"] + [f"w1.{o}" for o in range(1, ncols)], wsum2, [f"w2.{o}" for o in range(1, NY)], late=-60)

    def wsum3():
        t = w2r[0]
        for j in range(1, NY):
            t = t + w2r[j]
        for j in range(NK):
            w3[j, :rk] = t[j * rk:(j + 1) * rk]
            w3[j, rk:] = t[ry:]
        w3r[k] = w3[k]

    flow.msg("w3", "k", (rk + 8) * width * 4, lambda: w3.at[1 - k], lambda: w3r.at[k], lambda: w3r.at[1 - k], partner)
    flow.event("w3s", ["w2"] + [f"w2.{o}" for o in range(1, NY)], wsum3, ["w3"], late=-60)

    def wsum4():
        w4r[z] = w3r[0] + w3r[1]

    for o in range(1, nz):
        flow.msg(f"w4.{o}", "z+", (rk + 8) * width * 4,
                 lambda: w4r.at[z], lambda: w4r.at[z], lambda o=o: w4r.at[mod(z - o, nz)], zdev(o), slack=1.0)
    flow.event("w4s", ["w3s", "w3"], wsum4, [f"w4.{o}" for o in range(1, nz)], late=-60)

    def wsum5():
        t = w4r[0]
        for j in range(1, nz):
            t = t + w4r[j]
        t = t * scale
        wtot[c, y, k] = t[:rk]
        bg[...] = t[rk:rk + 1]

    flow.msg("w5", "k", rk * width * 4, lambda: wtot.at[c, y, k], lambda: wtot.at[c, y, k],
             lambda: wtot.at[c, y, 1 - k], partner)
    flow.event("w5s", ["w4s"] + [f"w4.{o}" for o in range(1, nz)], wsum5, ["w5"], late=-60)
    for o in range(1, NY):
        flow.msg(f"w6.{o}", "y+", ry * width * 4, lambda: wtot.at[c, y], lambda: wtot.at[c, y],
                 lambda o=o: wtot.at[c, mod(y - o, NY)], ydev(o), slack=0.5)
    flow.event("w6s", ["w5s", "w5"], None, [f"w6.{o}" for o in range(1, NY)], late=-60)
    for o in range(1, ncols):
        flow.msg(f"w7.{o}", "x", rx * width * 4, lambda: wtot.at[c], lambda: wtot.at[c],
                 lambda o=o: wtot.at[mod(c - o, ncols)], xdev(o), slack=0.5)
    flow.event("w7s", ["w6s"] + [f"w6.{o}" for o in range(1, NY)], None, [f"w7.{o}" for o in range(1, ncols)], late=-60)

    def wend():
        for a in range(ncols):
            for b in range(NY):
                for e in range(NK):
                    base = a * rx + b * ry + e * rk
                    wg[base:base + rk] = wtot[a, b, e]

    flow.event("wend", ["w7s"] + [f"w7.{o}" for o in range(1, ncols)], wend, late=30)
    flow.order()
    when = flow.done
    seq = sorted((max(when[ready0[dz, dy][side]], when[ready1[dz, dy][side]]), side, dz, dy)
                 for side in range(2) for dz in near_z for dy in near_y)
    seq = [(side, dz, dy) for _, side, dz, dy in seq]
    n_slots = len(seq) * cap
    n_src = 2 * ncols

    def owner(n):
        side, dz, dy = seq[n]
        return mod(z + dz, nz), mod(y + dy, NY), (1 - k if side else k)

    def links():
        ends = [jnp.int32(n_slots)] * n_src
        for n in range(len(seq)):
            o = rid(*owner(n))
            cnt = counts[o]
            for s in range(cap):
                src = src_ids[s, o]
                live = s < cnt
                p = ends[0]
                for j in range(1, n_src):
                    p = jnp.where(src == j, ends[j], p)
                prev[n * cap + s] = p
                for j in range(n_src):
                    ends[j] = jnp.where(jnp.logical_and(src == j, live), n * cap + s, ends[j])
        for j in range(n_src):
            last[j] = ends[j]
        sums[n_slots] = jnp.zeros((tile, width), F32)

    flow.event("links", ["ax.s.0", "ax.s.1"], links, cost=1.5, late=10)

    def backward(n0, n1):
        terms = []
        for n in range(n0, n1):
            zz, yy, kk = owner(n)
            o = rid(zz, yy, kk)
            g0 = ga[slot(kk, zz, yy), :tile, :]
            g1 = ga[slot(kk, zz, yy), tile:, :]
            for s in range(cap):
                g = jnp.where(dst_ids[s, o] == 0, g0, g1)
                terms.append(jnp.dot(av[o, s], g, preferred_element_type=F32))
        for i, t in enumerate(terms):
            i = n0 * cap + i
            sums[i] = t + sums[prev[i]]

    group = 2
    for n0 in range(0, len(seq), group):
        needs = ["links", "fw7"] + ([f"bw{n0 - group}"] if n0 else [])
        for n in range(n0, n0 + group):
            side, dz, dy = seq[n]
            needs += [ready0[dz, dy][side], ready1[dz, dy][side]]
        flow.event(f"bw{n0}", needs, lambda n0=n0: backward(n0, n0 + group), cost=0.35, late=20)
    bw_end = f"bw{len(seq) - group}"

    def grad_of(off, it, rows):
        return sums.at[last[2 * mod(c + off, ncols) + it]][rows, :]

    chain("sp", ncols, "x", xdev, [0, 1], tile,
          lambda off, it: sbuf.at[mod(c + off, ncols), it],
          None, srecv, lambda off, it: [bw_end],
          lambda it: grad.at[pl.ds(it * tile, tile)], grad_of)
    flow.event("settle", ["sp.fin.0", "sp.fin.1"], cost=0.0)
    flow.emit(send_sem, recv_sem)


N_MSGS = 288


def end_kernel(out, grad, wg, bg, weight, out_o, input_o, wg_o, bg_o):
    out_o[...] = out[...]
    input_o[...] = lax.dot_general(
        grad[...], weight[...], (((1,), (1,)), ((), ())), preferred_element_type=F32).astype(BF)
    wg_o[...] = wg[...]
    bg_o[...] = bg[...]


def solution(mesh):
    nrows, ncols = mesh.shape["rows"], mesh.shape["cols"]
    nz = nrows // (NK * NY)
    vmem = pl.BlockSpec(memory_space=pltpu.VMEM)
    smem = pl.BlockSpec(memory_space=pltpu.SMEM)
    anym = pl.BlockSpec(memory_space=pl.ANY)

    def local(features, weight, bias, tile_values, tile_source, tile_dest, send_counts, cotangent):
        owners, cap, tile = tile_values.shape[2:5]
        nodes, width = features.shape
        scale = 1.0 / math.sqrt(nodes * nrows * ncols)
        dims = (nz, ncols, tile, width, scale)
        tiles = tile_values.reshape(owners, cap, tile, tile)
        src_ids = jnp.transpose(tile_source, (0, 3, 1, 2)).reshape(cap, owners)
        dst_ids = jnp.transpose(tile_dest, (0, 3, 1, 2)).reshape(cap, owners)
        counts = send_counts.reshape(owners)
        rx = width // ncols
        ry, rk = rx // NY, rx // NY // NK
        hz, hy = nz // 2, NY // 2
        cut_f = (width * 3) // 8

        def body(*refs):
            main_kernel(dims, *refs)

        out, grad, wg, bg = pl.pallas_call(
            body,
            name="graph_main",
            out_shape=(
                jax.ShapeDtypeStruct((nodes, width), BF),
                jax.ShapeDtypeStruct((nodes, width), BF),
                jax.ShapeDtypeStruct((width, width), F32),
                jax.ShapeDtypeStruct((1, width), F32),
            ),
            in_specs=[vmem, vmem, vmem, anym, smem, smem, smem, vmem],
            out_specs=(vmem, vmem, vmem, vmem),
            scratch_shapes=[
                pltpu.VMEM((owners, cap, tile, tile), BF),
                pltpu.VMEM((ncols, nodes, width), BF),
                pltpu.VMEM((2 * ncols, width, tile), BF),
                pltpu.VMEM((nz, NY, width, 2 * tile), BF),
                pltpu.VMEM((nz, NY, width, 2 * tile), BF),
                pltpu.VMEM((nz, NY, cut_f, 2 * tile), BF),
                pltpu.VMEM((NY, nz, width - cut_f, 2 * tile), BF),
                pltpu.VMEM((2, hz, NY, cut_f, 2 * tile), BF),
                pltpu.VMEM((2, hy, nz, width - cut_f, 2 * tile), BF),
                pltpu.VMEM((2, hy, 1, cut_f, 2 * tile), BF),
                pltpu.VMEM((2, hz, 1, width - cut_f, 2 * tile), BF),
                pltpu.VMEM((width, 2 * tile), F32),
                pltpu.VMEM((ncols, rx + 8, width), F32),
                pltpu.VMEM((ncols, rx + 8, width), F32),
                pltpu.VMEM((NY, ry + 8, width), F32),
                pltpu.VMEM((NY, ry + 8, width), F32),
                pltpu.VMEM((NK, rk + 8, width), F32),
                pltpu.VMEM((NK, rk + 8, width), F32),
                pltpu.VMEM((nz, rk + 8, width), F32),
                pltpu.VMEM((ncols, NY, NK, rk, width), F32),
                pltpu.VMEM((nrows, nodes, width), BF),
                pltpu.VMEM((owners * cap + 1, tile, width), F32),
                pltpu.VMEM((ncols, 2, tile, width), BF),
                pltpu.VMEM((2, ncols // 2, 2, tile, width), BF),
                pltpu.SMEM((owners * cap,), jnp.int32),
                pltpu.SMEM((2 * ncols,), jnp.int32),
                pltpu.SemaphoreType.DMA((N_MSGS,)),
                pltpu.SemaphoreType.DMA((N_MSGS,)),
                pltpu.SemaphoreType.DMA((nz,)),
            ],
            compiler_params=pltpu.CompilerParams(
                collective_id=0, has_side_effects=True, vmem_limit_bytes=VMEM_LIMIT),
        )(features, weight, bias.reshape(1, width), tiles, src_ids, dst_ids, counts, cotangent)

        out, input_grad, wg, bg = pl.pallas_call(
            end_kernel,
            name="graph_end",
            out_shape=(
                jax.ShapeDtypeStruct((nodes, width), BF),
                jax.ShapeDtypeStruct((nodes, width), BF),
                jax.ShapeDtypeStruct((width, width), F32),
                jax.ShapeDtypeStruct((1, width), F32),
            ),
            in_specs=[vmem] * 5,
            out_specs=(vmem,) * 4,
        )(out, grad, wg, bg, weight)
        return out, input_grad, wg, bg.reshape(width)

    in_specs = (
        P(("rows", "cols"), None),
        P(),
        P(),
        P("rows", "cols", None, None, None, None),
        P("rows", "cols", None, None),
        P("rows", "cols", None, None),
        P("rows", "cols", None),
        P(("rows", "cols"), None),
    )
    out_specs = (P(("rows", "cols"), None), P(("rows", "cols"), None), P(), P())
    return jax.shard_map(local, mesh=mesh, in_specs=in_specs, out_specs=out_specs, check_vma=False)
```

```python
import math

import jax
import jax.numpy as jnp
from jax import lax
from jax.experimental import pallas as pl
from jax.experimental.pallas import tpu as pltpu
from jax.sharding import PartitionSpec as P

MESH = pl.DeviceIdType.MESH
BF = jnp.bfloat16
F32 = jnp.float32
NK = 2
NY = 4
VMEM_LIMIT = 63 * 1024 * 1024

RATE = {"x": 46e3, "y": 46e3, "z": 46e3, "k": 400e3}
BACKLOG = 1.6
DELAY = {"x": 2.4, "y": 2.8, "z": 2.8, "k": 1.0}


class Flow:
    def __init__(self):
        self.events = []
        self.msgs = {}

    def msg(self, name, link, nbytes, src, dst, view, peer, slack=0.0):
        self.msgs[name] = dict(idx=len(self.msgs), link=link, nbytes=nbytes, src=src, dst=dst, view=view,
                               peer=peer, slack=slack)

    def event(self, name, needs, fn=None, sends=(), cost=0.15, late=0):
        self.events.append((name, tuple(needs), fn, tuple(sends), cost, late))

    def order(self):
        done, free, now, out = {}, {}, 0.0, []
        pending = list(self.events)
        while pending:
            best = None
            for pos, ev in enumerate(pending):
                if all(n in done for n in ev[1]):
                    ready = max([now] + [done[n] for n in ev[1]]
                                + [free.get(self.msgs[m]["link"], 0.0) - BACKLOG for m in ev[3] if ev[5] > -50 and self.msgs[m]["link"] != "k"])
                    if best is None or (ready, ev[5], pos) < best:
                        best = (ready, ev[5], pos)
            ready, _, pos = best
            ev = pending.pop(pos)
            now = ready + ev[4]
            done[ev[0]] = now
            for s in ev[3]:
                m = self.msgs[s]
                end = max(now, free.get(m["link"], 0.0)) + m["nbytes"] / RATE[m["link"][0]]
                free[m["link"]] = end
                done[s] = end + DELAY[m["link"][0]] + m["slack"]
            out.append(ev)
        self.done = done
        return out

    def emit(self, send_sem, recv_sem):
        waited = set()

        def copy(m):
            return pltpu.make_async_remote_copy(
                src_ref=m["src"](), dst_ref=m["dst"](), send_sem=send_sem.at[m["idx"]],
                recv_sem=recv_sem.at[m["idx"]], device_id=m["peer"], device_id_type=MESH)

        for name, needs, fn, sends, _, _ in self.order():
            for n in needs:
                if n in self.msgs and n not in waited:
                    waited.add(n)
                    m = self.msgs[n]
                    v = m["view"]()
                    pltpu.make_async_remote_copy(
                        src_ref=v, dst_ref=v, send_sem=send_sem.at[m["idx"]],
                        recv_sem=recv_sem.at[m["idx"]], device_id=m["peer"], device_id_type=MESH).wait_recv()
            if fn is not None:
                fn()
            for s in sends:
                copy(self.msgs[s]).start()
        for n, m in self.msgs.items():
            copy(m).wait_send()


def greet(peers):
    barrier = pltpu.get_barrier_semaphore()
    for peer in peers:
        pl.semaphore_signal(barrier, inc=1, device_id=peer, device_id_type=MESH)
    pl.semaphore_wait(barrier, len(peers))


def mod(v, n):
    return lax.rem(v + 2 * n, n)


def main_kernel(dims, feat, weight, bias, tiles, src_ids, dst_ids, counts, cot,
                out, grad, wg, bg,
                av, xf, xt, psend, precv, own0, own1, r0, r1, s0, s1, qt,
                w1, w1r, w2, w2r, w3, w3r, w4r, wtot, ga, sums, sbuf, srecv, prev, last,
                send_sem, recv_sem, load_sem):
    nz, ncols, tile, width, scale = dims
    cap = av.shape[1]
    r = lax.axis_index("rows")
    c = lax.axis_index("cols")
    k = lax.rem(r, NK)
    y = lax.rem(lax.div(r, NK), NY)
    z = lax.div(r, NK * NY)
    hz, hy = nz // 2, NY // 2
    per_core = nz * NY

    def rid(zz, yy, kk):
        return (zz * NY + yy) * NK + kk

    def zdev(o):
        return (rid(mod(z + o, nz), y, k), c)

    def ydev(o):
        return (rid(z, mod(y + o, NY), k), c)

    def xdev(o):
        return (r, mod(c + o, ncols))

    partner = (rid(z, y, 1 - k), c)

    zord = [hz] + [s * d for d in range(hz - 1, 0, -1) for s in (1, -1)] + [0]
    yord = [hy] + [s * d for d in range(hy - 1, 0, -1) for s in (1, -1)] + [0]

    def load(i):
        zz = mod(z + zord[i], nz)
        blk = pl.ds(zz * NY * NK, NY * NK)
        return pltpu.make_async_copy(tiles.at[blk], av.at[blk], load_sem.at[i])

    for i in range(nz):
        load(i).start()

    greet([zdev(o) for o in range(1, nz)] + [ydev(o) for o in range(1, NY)]
          + [xdev(o) for o in range(1, ncols)] + [partner])

    flow = Flow()

    def gather(tag, n, link, dev, items, rows, view, ready, own=None, prio=4):
        h = n // 2
        piece = rows * width * 2
        part = {1: pl.ds(0, rows // 2), -1: pl.ds(rows // 2, rows // 2)}

        def cut(ref, d, i):
            return ref.at[part[d]] if i == h - 1 else ref

        for q, it in enumerate(items):
            for i in range(h):
                for d in (1, -1):
                    def src(i=i, d=d, it=it):
                        ref = own(it) if own is not None and i == 0 else view(-i * d, it)
                        return cut(ref, d, i)

                    flow.msg(f"{tag}.{i}.{d}.{q}", link + ("+" if d > 0 else "-"),
                             piece // 2 if i == h - 1 else piece, src,
                             lambda i=i, d=d, it=it: cut(view(-i * d, it), d, i),
                             lambda i=i, d=d, it=it: cut(view(-(i + 1) * d, it), d, i), dev(d))
            flow.event(f"{tag}.s.{q}", ready(it), None, [f"{tag}.0.1.{q}", f"{tag}.0.-1.{q}"], cost=0.02, late=prio)
            for i in range(h - 1):
                for d in (1, -1):
                    flow.event(f"{tag}.f{i}.{d}.{q}", [f"{tag}.{i}.{d}.{q}"], None, [f"{tag}.{i + 1}.{d}.{q}"], cost=0.02, late=prio + i + 1)
            flow.event(f"{tag}.last.{q}", [f"{tag}.{h - 1}.1.{q}", f"{tag}.{h - 1}.-1.{q}"], None, cost=0.02)

        def have(off, q, mine):
            off = off % n
            if off == 0:
                return mine
            if off == h:
                return f"{tag}.last.{q}"
            return f"{tag}.f{off - 1}.-1.{q}" if off < h else f"{tag}.f{n - off - 1}.1.{q}"

        return have

    def xrows(it):
        return pl.ds(it * tile, tile)

    have_x = gather("ax", ncols, "x", xdev, [0, 1], tile,
                    lambda off, it: xf.at[mod(c + off, ncols), xrows(it)], lambda it: [],
                    lambda it: feat.at[xrows(it)])
    xts = []
    for off in [0, 1, -1, ncols // 2]:
        for h in range(2):
            def turn(off=off, h=h):
                block = feat[h * tile:(h + 1) * tile, :] if off == 0 else xf[mod(c + off, ncols), h * tile:(h + 1) * tile, :]
                xt[2 * mod(c + off, ncols) + h] = block.T

            flow.event(f"xt{off}.{h}", [have_x(off, h, f"ax.s.{h}"), "ax.s.1"], turn, cost=0.2, late=5)
            xts.append(f"xt{off}.{h}")
    flow.event("xt", xts, cost=0.0)

    cut_f = (width * 3) // 8
    def partial_tile(o):
        lhs, rhs = [], []
        cnt = counts[o]
        for s in range(cap):
            t = dst_ids[s, o]
            live = jnp.where(s < cnt, 1, 0)
            m1 = (live * t).astype(F32)
            m0 = (live * (1 - t)).astype(F32)
            a = av[o, s]
            lhs.append(xt[src_ids[s, o]])
            rhs.append(jnp.concatenate(
                [a * jnp.full((tile, tile), m0, F32).astype(BF),
                 a * jnp.full((tile, tile), m1, F32).astype(BF)], axis=1))
        return jnp.dot(jnp.concatenate(lhs, axis=1), jnp.concatenate(rhs, axis=0),
                       preferred_element_type=F32).astype(BF)

    def forward(i, side):
        zz = mod(z + zord[i], nz)
        if side:
            load(i).wait()

        def body(jj, carry):
            for u in range(2):
                j = 2 * jj + u
                if side:
                    psend[zz, j] = partial_tile(rid(zz, j, 1 - k))
                else:
                    mine = partial_tile(rid(zz, j, k))
                    own0[zz, j] = mine[:cut_f]
                    own1[j, zz] = mine[cut_f:]
            return carry

        lax.fori_loop(0, NY // 2, body, 0)

    for i in range(nz):
        zat = lambda i=i: mod(z + zord[i], nz)
        flow.msg(f"pe{i}", "k", NY * 2 * width * tile * 2,
                 lambda f=zat: psend.at[f()], lambda f=zat: precv.at[f()], lambda f=zat: precv.at[f()], partner)
        flow.event(f"ft{i}", ["xt"] + ([f"fw{i - 1}"] if i else []), lambda i=i: forward(i, True), [f"pe{i}"], cost=0.65, late=20)
        flow.event(f"fw{i}", [f"ft{i}"], lambda i=i: forward(i, False), cost=0.65, late=20)

    def chain(tag, n, link, dev, items, length, buf, extra, rbuf, ready, final, value=None, prio=0, buf_cols=width):
        halves = {1: pl.ds(0, length // 2), -1: pl.ds(length // 2, length // 2)}
        h = n // 2
        piece = length * buf_cols * 2

        def rview(i, d, q, rows=None):
            v = rbuf.at[0 if d > 0 else 1, i, q]
            return v if rows is None else v.at[rows]

        def combine(off, it, recvs):
            for d in (1, -1):
                rows = halves[d]
                v = buf(off, it)[rows, :].astype(F32) if value is None else value(off, it, rows)
                e = extra(off, it) if extra is not None else None
                if e is not None:
                    v = v + e[rows, :].astype(F32)
                for (i, rd, q) in recvs:
                    if i > 0 or rd == d:
                        v = v + rview(i, rd, q)[rows, :].astype(F32)
                yield rows, v

        def store(off, it, recvs):
            dst = buf(off, it)
            for rows, v in combine(off, it, recvs):
                dst[rows, :] = v.astype(BF)

        for q, it in enumerate(items):
            for i in range(h):
                for d in (1, -1):
                    off = d * (h - i)
                    rows = halves[d] if i == 0 else None

                    def src(off=off, it=it, rows=rows):
                        v = buf(off, it)
                        return v if rows is None else v.at[rows]

                    def dst(i=i, d=d, q=q, rows=rows):
                        return rview(i, d, q, rows)

                    flow.msg(f"{tag}.{i}.{d}.{q}", link + ("+" if d > 0 else "-"),
                             piece // 2 if i == 0 else piece, src, dst, dst, dev(d))
            if extra is not None or value is not None:
                flow.event(f"{tag}.s0.{q}", ready(h, it), lambda it=it: store(h, it, ()),
                           [f"{tag}.0.1.{q}", f"{tag}.0.-1.{q}"], late=prio)
            else:
                flow.event(f"{tag}.s0.{q}", ready(h, it), None, [f"{tag}.0.1.{q}", f"{tag}.0.-1.{q}"], cost=0.02)
            for i in range(1, h):
                for d in (1, -1):
                    off = d * (h - i)
                    flow.event(f"{tag}.s{i}.{d}.{q}", list(ready(off, it)) + [f"{tag}.{i - 1}.{d}.{q}"],
                               lambda off=off, it=it, i=i, d=d, q=q: store(off, it, [(i - 1, d, q)]),
                               [f"{tag}.{i}.{d}.{q}"], late=prio + i)

            def finish(it=it, q=q):
                recvs = [(h - 1, 1, q), (h - 1, -1, q)]
                if final is None:
                    store(0, it, recvs)
                else:
                    for rows, v in combine(0, it, recvs):
                        final(it)[rows, :] = v.astype(final(it).dtype)

            flow.event(f"{tag}.fin.{q}", list(ready(0, it)) + [f"{tag}.{h - 1}.1.{q}", f"{tag}.{h - 1}.-1.{q}"], finish, late=prio)

    def zpos(off):
        return [i for i, v in enumerate(zord) if (v - off) % nz == 0][0]

    def ypos(off):
        return [i for i, v in enumerate(yord) if (v - off) % NY == 0][0]

    rows_lo, rows_hi = pl.ds(0, cut_f), pl.ds(cut_f, width - cut_f)
    chain("a1", nz, "z", zdev, yord, cut_f,
          lambda off, dy: own0.at[mod(z + off, nz), mod(y + dy, NY)],
          lambda off, dy: precv.at[mod(z + off, nz), mod(y + dy, NY), rows_lo],
          r0, lambda off, dy: [f"fw{zpos(off)}", f"pe{zpos(off)}"], None, prio=4)
    chain("b1", NY, "y", ydev, zord, width - cut_f,
          lambda off, dz: own1.at[mod(y + off, NY), mod(z + dz, nz)],
          lambda off, dz: precv.at[mod(z + dz, nz), mod(y + off, NY), rows_hi],
          r1, lambda off, dz: [f"fw{zpos(dz)}", f"pe{zpos(dz)}"], None, prio=4)
    chain("b2", nz, "z", zdev, [0], width - cut_f,
          lambda off, it: own1.at[y, mod(z + off, nz)],
          None, s1, lambda off, it: [f"b1.fin.{zpos(off)}"], lambda it: qt.at[rows_hi])
    chain("a2", NY, "y", ydev, [0], cut_f,
          lambda off, it: own0.at[z, mod(y + off, NY)],
          None, s0, lambda off, it: [f"a1.fin.{ypos(off)}"], lambda it: qt.at[rows_lo])

    slot = lambda kk, zz, yy: kk * per_core + zz * NY + yy

    def activate(t):
        rows = slice(t * tile, (t + 1) * tile)
        wb = weight[...]
        q = qt[:, rows]
        qh = q.astype(BF)
        ql = (q - qh.astype(F32)).astype(BF)
        dn = (((0,), (0,)), ((), ()))
        pre = (lax.dot_general(qh, wb, dn, preferred_element_type=F32)
               + lax.dot_general(ql, wb, dn, preferred_element_type=F32) + bias[...])
        ks = math.sqrt(2.0 / math.pi)
        sq = pre * pre
        th = jnp.tanh(ks * pre * (1.0 + 0.044715 * sq))
        slope = 0.5 * (1.0 + th) + 0.5 * pre * (1.0 - th * th) * (ks * (1.0 + 3 * 0.044715 * sq))
        ga[slot(k, z, y), rows, :] = (cot[rows, :].astype(F32) * slope).astype(BF)
        out[rows, :] = (0.5 * pre * (1.0 + th)).astype(BF)

    flow.event("act0", ["a2.fin.0", "b2.fin.0"], lambda: activate(0), cost=0.8)
    flow.event("act1", ["act0"], lambda: activate(1), cost=0.8)
    flow.event("act", ["act0", "act1"], cost=0.0)

    cut_a = (tile * 3) // 4
    rows_a, rows_b = pl.ds(0, cut_a), pl.ds(cut_a, 2 * tile - cut_a)
    len_b = 2 * tile - cut_a

    def gview(kk, dz, dy, rows):
        return ga.at[slot(kk, mod(z + dz, nz), mod(y + dy, NY)), rows]

    have_a1 = gather("ga1", NY, "y", ydev, [0], cut_a,
                     lambda off, it: gview(k, 0, off, rows_a), lambda it: ["act0"], prio=-4)
    have_b1 = gather("gb1", nz, "z", zdev, [0], len_b,
                     lambda off, it: gview(k, off, 0, rows_b), lambda it: ["act"], prio=-8)
    near_y, near_z = yord[::-1], zord[::-1]
    have_a2 = gather("ga2", nz, "z", zdev, near_y, cut_a,
                     lambda off, dy: gview(k, off, dy, rows_a), lambda dy: [have_a1(dy, 0, "act0")])
    have_b2 = gather("gb2", NY, "y", ydev, near_z, len_b,
                     lambda off, dz: gview(k, dz, off, rows_b), lambda dz: [have_b1(dz, 0, "act")])
    ready0, ready1 = {}, {}
    for dz in near_z:
        for dy in near_y:
            have = have_a2(dz, near_y.index(dy), have_a1(dy, 0, "act0"))
            mine = lambda dz=dz, dy=dy: gview(k, dz, dy, rows_a)
            other = lambda dz=dz, dy=dy: gview(1 - k, dz, dy, rows_a)
            flow.msg(f"ka{dz}.{dy}", "k", cut_a * width * 2, mine, mine, other, partner)
            flow.event(f"kas{dz}.{dy}", [have], None, [f"ka{dz}.{dy}"], cost=0.02)
            ready0[dz, dy] = (have, f"ka{dz}.{dy}")
            have = have_b2(dy, near_z.index(dz), have_b1(dz, 0, "act"))
            mine = lambda dz=dz, dy=dy: gview(k, dz, dy, rows_b)
            other = lambda dz=dz, dy=dy: gview(1 - k, dz, dy, rows_b)
            flow.msg(f"kb{dz}.{dy}", "k", len_b * width * 2, mine, mine, other, partner)
            flow.event(f"kbs{dz}.{dy}", [have], None, [f"kb{dz}.{dy}"], cost=0.02)
            ready1[dz, dy] = (have, f"kb{dz}.{dy}")

    rx, ry, rk = width // ncols, width // ncols // NY, width // ncols // NY // NK

    def wpart():
        q = qt[...].astype(BF)
        g = ga[slot(k, z, y)]
        w = jnp.dot(q, g, preferred_element_type=F32)
        b = jnp.broadcast_to(jnp.sum(g.astype(F32), axis=0, keepdims=True), (8, width))
        for j in range(ncols):
            w1[j, :rx] = w[j * rx:(j + 1) * rx]
            w1[j, rx:] = b
        w1r[c] = w1[c]

    for o in range(1, ncols):
        flow.msg(f"w1.{o}", "x", (rx + 8) * width * 4,
                 lambda o=o: w1.at[mod(c + o, ncols)], lambda: w1r.at[c], lambda o=o: w1r.at[mod(c - o, ncols)], xdev(o), slack=0.5)
    flow.event("w1", ["act", "ga1.s.0", "gb1.s.0", "ga2.s.0", "gb2.s.0"], wpart,
               [f"w1.{o}" for o in range(1, ncols)], cost=1.2, late=15)

    def wsum2():
        t = w1r[0]
        for j in range(1, ncols):
            t = t + w1r[j]
        for j in range(NY):
            w2[j, :ry] = t[j * ry:(j + 1) * ry]
            w2[j, ry:] = t[rx:]
        w2r[y] = w2[y]

    for o in range(1, NY):
        flow.msg(f"w2.{o}", "y+", (ry + 8) * width * 4,
                 lambda o=o: w2.at[mod(y + o, NY)], lambda: w2r.at[y], lambda o=o: w2r.at[mod(y - o, NY)], ydev(o), slack=0.5)
    flow.event("w2", ["w1"] + [f"w1.{o}" for o in range(1, ncols)], wsum2, [f"w2.{o}" for o in range(1, NY)], late=-60)

    def wsum3():
        t = w2r[0]
        for j in range(1, NY):
            t = t + w2r[j]
        for j in range(NK):
            w3[j, :rk] = t[j * rk:(j + 1) * rk]
            w3[j, rk:] = t[ry:]
        w3r[k] = w3[k]

    flow.msg("w3", "k", (rk + 8) * width * 4, lambda: w3.at[1 - k], lambda: w3r.at[k], lambda: w3r.at[1 - k], partner)
    flow.event("w3s", ["w2"] + [f"w2.{o}" for o in range(1, NY)], wsum3, ["w3"], late=-60)

    def wsum4():
        w4r[z] = w3r[0] + w3r[1]

    for o in range(1, nz):
        flow.msg(f"w4.{o}", "z+", (rk + 8) * width * 4,
                 lambda: w4r.at[z], lambda: w4r.at[z], lambda o=o: w4r.at[mod(z - o, nz)], zdev(o), slack=1.0)
    flow.event("w4s", ["w3s", "w3"], wsum4, [f"w4.{o}" for o in range(1, nz)], late=-60)

    def wsum5():
        t = w4r[0]
        for j in range(1, nz):
            t = t + w4r[j]
        t = t * scale
        wtot[c, y, k] = t[:rk]
        bg[...] = t[rk:rk + 1]

    flow.msg("w5", "k", rk * width * 4, lambda: wtot.at[c, y, k], lambda: wtot.at[c, y, k],
             lambda: wtot.at[c, y, 1 - k], partner)
    flow.event("w5s", ["w4s"] + [f"w4.{o}" for o in range(1, nz)], wsum5, ["w5"], late=-60)
    for o in range(1, NY):
        flow.msg(f"w6.{o}", "y+", ry * width * 4, lambda: wtot.at[c, y], lambda: wtot.at[c, y],
                 lambda o=o: wtot.at[c, mod(y - o, NY)], ydev(o), slack=0.5)
    flow.event("w6s", ["w5s", "w5"], None, [f"w6.{o}" for o in range(1, NY)], late=-60)
    for o in range(1, ncols):
        flow.msg(f"w7.{o}", "x", rx * width * 4, lambda: wtot.at[c], lambda: wtot.at[c],
                 lambda o=o: wtot.at[mod(c - o, ncols)], xdev(o), slack=0.5)
    flow.event("w7s", ["w6s"] + [f"w6.{o}" for o in range(1, NY)], None, [f"w7.{o}" for o in range(1, ncols)], late=-60)

    def wend():
        for a in range(ncols):
            for b in range(NY):
                for e in range(NK):
                    base = a * rx + b * ry + e * rk
                    wg[base:base + rk] = wtot[a, b, e]

    flow.event("wend", ["w7s"] + [f"w7.{o}" for o in range(1, ncols)], wend, late=30)
    flow.order()
    when = flow.done
    seq = sorted((max(when[ready0[dz, dy][side]], when[ready1[dz, dy][side]]), side, dz, dy)
                 for side in range(2) for dz in near_z for dy in near_y)
    seq = [(side, dz, dy) for _, side, dz, dy in seq]
    n_slots = len(seq) * cap
    n_src = 2 * ncols

    def owner(n):
        side, dz, dy = seq[n]
        return mod(z + dz, nz), mod(y + dy, NY), (1 - k if side else k)

    ends = [None] * n_src
    share = len(seq) // 8

    def links(part):
        if part == 0:
            ends[:] = [jnp.int32(n_slots)] * n_src
            sums[n_slots] = jnp.zeros((tile, width), F32)
        for n in range(part * share, (part + 1) * share):
            o = rid(*owner(n))
            cnt = counts[o]
            for s in range(cap):
                src = jnp.where(s < cnt, src_ids[s, o], n_src)
                p = ends[0]
                for j in range(1, n_src):
                    p = jnp.where(src == j, ends[j], p)
                prev[n * cap + s] = p
                for j in range(n_src):
                    ends[j] = jnp.where(src == j, n * cap + s, ends[j])
        if part == 7:
            for j in range(n_src):
                last[j] = ends[j]

    for part in range(8):
        flow.event(f"links{part}", ["ax.s.0", "ax.s.1"] + ([f"links{part - 1}"] if part else []),
                   lambda part=part: links(part), cost=0.6, late=25)

    def backward(n0, n1):
        terms = []
        for n in range(n0, n1):
            zz, yy, kk = owner(n)
            o = rid(zz, yy, kk)
            g0 = ga[slot(kk, zz, yy), :tile, :]
            g1 = ga[slot(kk, zz, yy), tile:, :]
            for s in range(cap):
                g = jnp.where(dst_ids[s, o] == 0, g0, g1)
                terms.append(jnp.dot(av[o, s], g, preferred_element_type=F32))
        for i, t in enumerate(terms):
            i = n0 * cap + i
            sums[i] = t + sums[prev[i]]

    group = 2
    for n0 in range(0, len(seq), group):
        needs = ["links7", "fw7"] + ([f"bw{n0 - group}"] if n0 else [])
        for n in range(n0, n0 + group):
            side, dz, dy = seq[n]
            needs += [ready0[dz, dy][side], ready1[dz, dy][side]]
        flow.event(f"bw{n0}", needs, lambda n0=n0: backward(n0, n0 + group), cost=0.35, late=20)
    bw_end = f"bw{len(seq) - group}"

    def grad_of(off, it, rows):
        return sums.at[last[2 * mod(c + off, ncols) + it]][rows, :]

    chain("sp", ncols, "x", xdev, [0, 1], tile,
          lambda off, it: sbuf.at[mod(c + off, ncols), it],
          None, srecv, lambda off, it: [bw_end],
          lambda it: grad.at[pl.ds(it * tile, tile)], grad_of)
    flow.event("settle", ["sp.fin.0", "sp.fin.1"], cost=0.0)
    flow.emit(send_sem, recv_sem)


N_MSGS = 288


def end_kernel(out, grad, wg, bg, weight, out_o, input_o, wg_o, bg_o):
    out_o[...] = out[...]
    input_o[...] = lax.dot_general(
        grad[...], weight[...], (((1,), (1,)), ((), ())), preferred_element_type=F32).astype(BF)
    wg_o[...] = wg[...]
    bg_o[...] = bg[...]


def solution(mesh):
    nrows, ncols = mesh.shape["rows"], mesh.shape["cols"]
    nz = nrows // (NK * NY)
    vmem = pl.BlockSpec(memory_space=pltpu.VMEM)
    smem = pl.BlockSpec(memory_space=pltpu.SMEM)
    anym = pl.BlockSpec(memory_space=pl.ANY)

    def local(features, weight, bias, tile_values, tile_source, tile_dest, send_counts, cotangent):
        owners, cap, tile = tile_values.shape[2:5]
        nodes, width = features.shape
        scale = 1.0 / math.sqrt(nodes * nrows * ncols)
        dims = (nz, ncols, tile, width, scale)
        tiles = tile_values.reshape(owners, cap, tile, tile)
        src_ids = jnp.transpose(tile_source, (0, 3, 1, 2)).reshape(cap, owners)
        dst_ids = jnp.transpose(tile_dest, (0, 3, 1, 2)).reshape(cap, owners)
        counts = send_counts.reshape(owners)
        rx = width // ncols
        ry, rk = rx // NY, rx // NY // NK
        hz, hy = nz // 2, NY // 2
        cut_f = (width * 3) // 8

        def body(*refs):
            main_kernel(dims, *refs)

        out, grad, wg, bg = pl.pallas_call(
            body,
            name="graph_main",
            out_shape=(
                jax.ShapeDtypeStruct((nodes, width), BF),
                jax.ShapeDtypeStruct((nodes, width), BF),
                jax.ShapeDtypeStruct((width, width), F32),
                jax.ShapeDtypeStruct((1, width), F32),
            ),
            in_specs=[vmem, vmem, vmem, anym, smem, smem, smem, vmem],
            out_specs=(vmem, vmem, vmem, vmem),
            scratch_shapes=[
                pltpu.VMEM((owners, cap, tile, tile), BF),
                pltpu.VMEM((ncols, nodes, width), BF),
                pltpu.VMEM((2 * ncols, width, tile), BF),
                pltpu.VMEM((nz, NY, width, 2 * tile), BF),
                pltpu.VMEM((nz, NY, width, 2 * tile), BF),
                pltpu.VMEM((nz, NY, cut_f, 2 * tile), BF),
                pltpu.VMEM((NY, nz, width - cut_f, 2 * tile), BF),
                pltpu.VMEM((2, hz, NY, cut_f, 2 * tile), BF),
                pltpu.VMEM((2, hy, nz, width - cut_f, 2 * tile), BF),
                pltpu.VMEM((2, hy, 1, cut_f, 2 * tile), BF),
                pltpu.VMEM((2, hz, 1, width - cut_f, 2 * tile), BF),
                pltpu.VMEM((width, 2 * tile), F32),
                pltpu.VMEM((ncols, rx + 8, width), F32),
                pltpu.VMEM((ncols, rx + 8, width), F32),
                pltpu.VMEM((NY, ry + 8, width), F32),
                pltpu.VMEM((NY, ry + 8, width), F32),
                pltpu.VMEM((NK, rk + 8, width), F32),
                pltpu.VMEM((NK, rk + 8, width), F32),
                pltpu.VMEM((nz, rk + 8, width), F32),
                pltpu.VMEM((ncols, NY, NK, rk, width), F32),
                pltpu.VMEM((nrows, nodes, width), BF),
                pltpu.VMEM((owners * cap + 1, tile, width), F32),
                pltpu.VMEM((ncols, 2, tile, width), BF),
                pltpu.VMEM((2, ncols // 2, 2, tile, width), BF),
                pltpu.SMEM((owners * cap,), jnp.int32),
                pltpu.SMEM((2 * ncols,), jnp.int32),
                pltpu.SemaphoreType.DMA((N_MSGS,)),
                pltpu.SemaphoreType.DMA((N_MSGS,)),
                pltpu.SemaphoreType.DMA((nz,)),
            ],
            compiler_params=pltpu.CompilerParams(
                collective_id=0, has_side_effects=True, vmem_limit_bytes=VMEM_LIMIT),
        )(features, weight, bias.reshape(1, width), tiles, src_ids, dst_ids, counts, cotangent)

        out, input_grad, wg, bg = pl.pallas_call(
            end_kernel,
            name="graph_end",
            out_shape=(
                jax.ShapeDtypeStruct((nodes, width), BF),
                jax.ShapeDtypeStruct((nodes, width), BF),
                jax.ShapeDtypeStruct((width, width), F32),
                jax.ShapeDtypeStruct((1, width), F32),
            ),
            in_specs=[vmem] * 5,
            out_specs=(vmem,) * 4,
        )(out, grad, wg, bg, weight)
        return out, input_grad, wg, bg.reshape(width)

    in_specs = (
        P(("rows", "cols"), None),
        P(),
        P(),
        P("rows", "cols", None, None, None, None),
        P("rows", "cols", None, None),
        P("rows", "cols", None, None),
        P("rows", "cols", None),
        P(("rows", "cols"), None),
    )
    out_specs = (P(("rows", "cols"), None), P(("rows", "cols"), None), P(), P())
    return jax.shard_map(local, mesh=mesh, in_specs=in_specs, out_specs=out_specs, check_vma=False)
```
